512 devices in a mesh: lat: 64 (over x, z, core), fld: 8 (over y).
Axes of the slice: x: 4, y: 8, z: 8, core: 2. Of those that a mesh axis runs over, the one named last changes fastest.
Arguments:
- fields: bfloat16 [16, 2048, 8192], P('fld', 'lat'), may hold values from -6 to 6
- legendre: bfloat16 [256, 2, 1024, 1024], P('lat', None, 'fld'), may hold values from -0.1875 to 0.1875
- damping: float32 [16], replicated, may hold values from 0.5 to 30
- assignment: int32 [256], replicated, may hold values from 0 to 255, each once
- truncation: int32 [256], replicated, may hold values from 512 to 2048, as said below
Outputs:
- field_out: bfloat16 [16, 2048, 8192], P('fld', 'lat')
- spectra: bfloat16 [256, 2, 16, 2, 1024], P('lat', None, None, None, 'fld')
The draws below stay inside these ranges and needn't reach their ends.
Inputs may be any that keep to these rules, and one draw needn't show every extreme that they name: `assignment`: a permutation of the wavenumber indices. truncation[0] is 2048 and truncation[255] is 512.
All inputs are finite; a program needn't handle non-finite values.
Results may differ from the reference program's by a relative error of at most 0.009.
Values may be sent and summed in bfloat16 or wider, within the bound.
No kernel may reach another device: no remote copies, remote signals or barrier semaphores. Data moves between devices by JAX's collectives and lax.ppermute only.
A program may use at most 64 MiB of HBM per device.

```python
import math
import jax
import jax.numpy as jnp
from jax import lax

NLON = 8192
NLAT = 2048
NDEG = 2048
NHALF = 1024
HALF_DEG = 1024
WAVES = 256
FIELDS = 16


def draw_truncation(key, part):
    wave_index = jnp.arange(WAVES, dtype=jnp.int32)
    baseline = NDEG - 3 * NDEG // 4 * wave_index // (WAVES - 1)
    jitter = jax.random.randint(jax.random.fold_in(key, 7), (WAVES,), -(NDEG // 16), NDEG // 16 + 1, dtype=jnp.int32)
    at_ends = (wave_index == 0) | (wave_index == WAVES - 1)
    jitter = jnp.where(at_ends, 0, jitter)
    return jnp.clip(baseline + jitter, NDEG // 4, NDEG).astype(jnp.int32)


def block_scale(own_key, dims, pieces, smallest, top_value):
    loudness, own = 1.0, jax.random.fold_in(own_key, 6)
    for axis_at, blocks in pieces:
        steps = jnp.exp(jax.random.uniform(jax.random.fold_in(own, axis_at), (blocks,), jnp.float32, smallest / len(pieces), top_value / len(pieces)))
        loudness = loudness * jnp.repeat(steps, dims[axis_at] // blocks).reshape([-1 if axis == axis_at else 1 for axis in range(len(dims))])
    return loudness


def gaussian(rng, shape, deviation, bound, cuts=(), held_as=jnp.bfloat16):
    array = jax.random.normal(rng, shape, jnp.float32) * deviation
    if len(cuts) > 0:
        array = block_scale(rng, shape, cuts, -0.22, 0.18) * array
    return jnp.clip(array, min=-bound, max=bound).astype(held_as)


def setup_inputs(seed: int = 0) -> dict:
    streams_of = jax.random.split(jax.random.key(seed), 6)
    return {
        "fields": gaussian(streams_of[0], (FIELDS, NLAT, NLON), 1.0, 6.0, ((0, 8), (1, 64))),
        "legendre": gaussian(streams_of[1], (WAVES, 2, HALF_DEG, NHALF), NHALF ** -0.5, 0.1875, ((0, 64), (2, 8))),
        "damping": jnp.clip(jnp.exp(jax.random.uniform(streams_of[2], (FIELDS,), jnp.float32, math.log(0.5), math.log(30.0))), 0.5, 30.0),
        "assignment": jax.random.permutation(streams_of[3], WAVES).astype(jnp.int32),
        "truncation": draw_truncation(jax.random.fold_in(streams_of[5], 71), 0),
    }


def basis_table(wave_numbers, lon_count):
    positions = jnp.arange(lon_count, dtype=jnp.int32)
    phase = wave_numbers[:, None] * positions[None, :] % lon_count
    angles = phase.astype(jnp.float32) * (2.0 * math.pi / lon_count)
    factor = math.sqrt(2.0 / lon_count)
    return jnp.stack([factor * jnp.cos(angles), -factor * jnp.sin(angles)]).astype(jnp.bfloat16)

def reference(fields, legendre, damping, assignment, truncation):
    highest = lax.Precision.HIGHEST
    fourier_basis = basis_table(assignment.astype(jnp.int32) + 1, NLON)
    basis_wide = fourier_basis.astype(jnp.float32)

    def forward(one_field):
        squared = lax.optimization_barrier((one_field.astype(jnp.float32) ** 2).astype(jnp.bfloat16))
        return jnp.einsum('lx,rjx->ljr', squared.astype(jnp.float32), basis_wide, precision=highest).astype(jnp.bfloat16)
    fourier = lax.map(forward, fields)
    northern = fourier[:, :NHALF].astype(jnp.float32)
    southern = fourier[:, NHALF:].astype(jnp.float32)
    folded = jnp.stack([(northern + southern) * 0.5, (northern - southern) * 0.5], axis=1).astype(jnp.bfloat16)
    by_slot = jnp.transpose(folded, (3, 1, 0, 4, 2))
    top_degree = WAVES + NDEG - 1
    pair_index = jnp.arange(HALF_DEG, dtype=jnp.int32)
    parity = jnp.arange(2, dtype=jnp.int32)
    degree_offset = 2 * pair_index[None, :] + parity[:, None]
    slot_limits = jnp.take(truncation, assignment, axis=0)

    def per_slot(inputs):
        table, folded_slot, limit, wave_index = inputs
        table_wide = table.astype(jnp.float32)
        coefficient = jnp.einsum('aql,afrl->afrq', table_wide, folded_slot.astype(jnp.float32), precision=highest)
        degree = (wave_index + 1 + degree_offset).astype(jnp.float32)
        degree_ratio = degree * (degree + 1.0) / float(top_degree * (top_degree + 1))
        kept_mask = degree_offset < limit
        scaled = coefficient / (1.0 + damping[None, :, None, None] * (degree_ratio * degree_ratio)[:, None, None, :])
        diffused = jnp.where(kept_mask[:, None, None, :], scaled, 0.0).astype(jnp.bfloat16)
        synthesis = jnp.einsum('afrq,aql->afrl', diffused.astype(jnp.float32), table_wide, precision=highest).astype(jnp.bfloat16)
        return (diffused, synthesis)
    spectra, synthesis_all = lax.map(per_slot, (legendre, by_slot, slot_limits, assignment.astype(jnp.int32)))
    sym_part = synthesis_all[:, 0].astype(jnp.float32)
    anti_part = synthesis_all[:, 1].astype(jnp.float32)
    grid_rows = jnp.concatenate([sym_part + anti_part, sym_part - anti_part], axis=-1).astype(jnp.bfloat16)
    per_field = jnp.transpose(grid_rows, (1, 0, 2, 3))

    def inverse(rows_field):
        return jnp.einsum('jrl,rjx->lx', rows_field.astype(jnp.float32), basis_wide, precision=highest).astype(jnp.bfloat16)
    field_out = lax.map(inverse, per_field)
    return (field_out, spectra)
```

```python
import math

import jax
import jax.numpy as jnp
import numpy as np
from jax import lax
from jax.experimental import pallas as pl
from jax.experimental.pallas import tpu as pltpu
from jax.sharding import PartitionSpec as P

F32 = jnp.float32
BF16 = jnp.bfloat16
RADIX = 8
HALF_ROOT = math.sqrt(0.5)
NT = (((1,), (1,)), ((), ()))
NN = (((1,), (0,)), ((), ()))
CLASS_ORDER = (1, 7, 2, 6, 3, 5, 8, 4)


def dot(a, b, dims):
    return lax.dot_general(a, b, dims, preferred_element_type=F32)


def wave_tables(total_waves, lon_count):
    span = lon_count // RADIX
    per = total_waves // RADIX
    waves = np.concatenate([RADIX * np.arange(per) + c for c in CLASS_ORDER])
    phase = (waves[:, None] * np.arange(span)[None, :]) % lon_count
    angle = phase * (2.0 * np.pi / lon_count)
    sign = np.repeat([1.0, -1.0, 1.0, -1.0, 1.0, -1.0, 1.0, 1.0], per)[:, None]
    factor = math.sqrt(2.0 / lon_count)
    return (
        jnp.asarray((factor * np.cos(angle)).astype(np.float32), BF16),
        jnp.asarray((factor * sign * np.sin(angle)).astype(np.float32), BF16),
    )


def wave_select(assign_row, total_waves):
    per = total_waves // RADIX
    row = lax.broadcasted_iota(jnp.int32, (total_waves, total_waves), 0)
    block = row // per
    cls = jnp.full_like(row, CLASS_ORDER[0])
    for b in range(1, RADIX):
        cls = jnp.where(block == b, CLASS_ORDER[b], cls)
    wave = RADIX * (row % per) + cls - 1
    return jnp.where(wave == assign_row, 1.0, 0.0).astype(BF16)


def forward_kernel(fields_ref, assign_ref, cos_ref, sin_ref, out_ref, z_ref):
    rows, lon_count = fields_ref.shape
    waves, span = cos_ref.shape
    per = waves // RADIX
    tile = 16
    width = 256

    def fold_rows(step, carry):
        r0 = pl.multiple_of(step * tile, tile)
        for x0 in range(0, span, width):
            s = []
            for b in range(RADIX):
                v = fields_ref[pl.ds(r0, tile), b * span + x0 : b * span + x0 + width].astype(F32)
                s.append(v * v)
            e = [s[b] + s[b + 4] for b in range(4)]
            o = [s[b] - s[b + 4] for b in range(4)]
            u = HALF_ROOT * (o[1] - o[3])
            v = HALF_ROOT * (o[1] + o[3])
            even = e[0] + e[2]
            odd = e[1] + e[3]
            parts = (
                o[0] + u, -(o[2] + v),
                e[0] - e[2], e[3] - e[1],
                o[0] - u, o[2] - v,
                even + odd, even - odd,
            )
            for n, part in enumerate(parts):
                z_ref[n, pl.ds(r0, tile), x0 : x0 + width] = part.astype(BF16)
        return carry

    lax.fori_loop(0, rows // tile, fold_rows, 0)
    select = wave_select(assign_ref[...], waves)
    acc = jnp.zeros((2 * rows, waves), F32)
    for p in range(3):
        i0 = 2 * p * per
        zz = z_ref[2 * p : 2 * p + 2].reshape(2 * rows, span)
        dc = dot(zz, cos_ref[i0 : i0 + 2 * per, :], NT)
        ds = dot(zz, sin_ref[i0 : i0 + 2 * per, :], NT)
        real = dc[:rows] + ds[rows:]
        imag = dc[rows:] - ds[:rows]
        lane = lax.broadcasted_iota(jnp.int32, imag.shape, 1)
        imag = jnp.where(lane < per, imag, -imag)
        both = jnp.concatenate([real, imag], axis=0).astype(BF16)
        acc = acc + dot(both, select[i0 : i0 + 2 * per, :], NN)
    for p in range(2):
        i0 = (6 + p) * per
        z = z_ref[6 + p]
        real = dot(z, cos_ref[i0 : i0 + per, :], NT)
        imag = -dot(z, sin_ref[i0 : i0 + per, :], NT)
        both = jnp.concatenate([real, imag], axis=0).astype(BF16)
        acc = acc + dot(both, select[i0 : i0 + per, :], NN)
    out_ref[...] = acc.T.astype(BF16)


def fold_kernel(in_ref, out_ref, x_ref):
    copies = out_ref.shape[0]
    total = in_ref.shape[0]
    slots = 4
    half = total // 2
    x_ref[...] = in_ref[...].astype(F32)
    block = lax.broadcasted_iota(jnp.int32, (8, 128), 1) // 32
    for s in range(slots):
        folded = ([], [])
        for part in range(4):
            north = x_ref[pl.ds(4 * part + s, 8, stride=16), :]
            south = x_ref[pl.ds(half + 4 * part + s, 8, stride=16), :]
            folded[0].append((north + south) * 0.5)
            folded[1].append((north - south) * 0.5)
        for f in range(2):
            for r in range(2):
                source = 2 * r + f
                pair = []
                for a in range(2):
                    rows = None
                    for part in range(4):
                        shift = (32 * (part - source)) % 128
                        moved = folded[a][part]
                        if shift:
                            moved = pltpu.roll(moved, shift, 1)
                        rows = moved if rows is None else jnp.where(block == part, moved, rows)
                    pair.append(rows)
                tile = jnp.concatenate(pair, axis=0).astype(BF16)
                row = ((2 * f + r) * 8 + 2 * s) * 8
                for copy in range(copies):
                    out_ref[copy, row : row + 16, :] = tile


def legendre_kernel(x_ref, table_ref, damping_ref, assign_ref, limit_ref, spectra_ref, out_ref, wide_ref, sums_ref, *, top):
    pairs, degrees, half_lat = table_ref.shape
    columns = spectra_ref.shape[1]
    slots = pairs // 2
    groups = half_lat // 128
    stride = pairs * groups
    slot0 = lax.axis_index("lat") * slots
    first = lax.axis_index("fld") * degrees
    wide_ref[...] = x_ref[...].astype(F32)
    field = lax.broadcasted_iota(jnp.int32, (columns, degrees), 0) // 2
    damp = jnp.zeros((columns, degrees), F32)
    for n in range(columns // 2):
        damp = jnp.where(field == n, damping_ref[n], damp)
    pair_index = first + lax.broadcasted_iota(jnp.int32, (columns, degrees), 1)
    for s in range(slots):
        wave = assign_ref[slot0 + s]
        limit = limit_ref[wave]
        for a in range(2):
            sa = 2 * s + a
            rows = jnp.concatenate(
                [wide_ref[pl.ds(sa * groups + g, columns, stride=stride), :] for g in range(groups)], axis=1
            ).astype(BF16)
            table = table_ref[sa]
            coefficient = dot(rows, table, NT)
            offset = 2 * pair_index + a
            degree = (wave + 1 + offset).astype(F32)
            ratio = degree * (degree + 1.0) / float(top * (top + 1))
            scaled = coefficient / (1.0 + damp * (ratio * ratio))
            diffused = jnp.where(offset < limit, scaled, 0.0).astype(BF16)
            spectra_ref[sa] = diffused
            back = dot(diffused, table, NN)
            for g in range(groups):
                sums_ref[pl.ds(sa * groups + g, columns, stride=stride), :] = back[:, g * 128 : g * 128 + 128]
    out_ref[...] = sums_ref[...].astype(BF16)


def unfold_kernel(in_ref, out_ref, y_ref):
    sources, total, _ = in_ref.shape
    half = total // 2
    block = lax.broadcasted_iota(jnp.int32, (8, 128), 1) // 32

    def summed(row):
        acc = in_ref[0, row : row + 16, :].astype(F32)
        for n in range(1, sources):
            acc = acc + in_ref[n, row : row + 16, :].astype(F32)
        return acc.astype(BF16).astype(F32)

    for s in range(4):
        north, south = {}, {}
        for f in range(2):
            for r in range(2):
                both = summed(((2 * f + r) * 8 + 2 * s) * 8)
                north[2 * r + f] = both[:8] + both[8:]
                south[2 * r + f] = both[:8] - both[8:]
        for part in range(4):
            for base, rows_of in ((0, north), (half, south)):
                rows = None
                for target in range(4):
                    shift = (32 * (target - part)) % 128
                    moved = rows_of[target]
                    if shift:
                        moved = pltpu.roll(moved, shift, 1)
                    rows = moved if rows is None else jnp.where(block == target, moved, rows)
                y_ref[pl.ds(base + 4 * part + s, 8, stride=16), :] = rows
    out_ref[...] = y_ref[...].astype(BF16)


def inverse_kernel(in_ref, assign_ref, cos_ref, sin_ref, out_ref, w_ref):
    rows, lon_count = out_ref.shape
    waves, span = cos_ref.shape
    per = waves // RADIX
    select = wave_select(assign_ref[...], waves)
    slots = in_ref[...].astype(F32).T.astype(BF16)

    def ordered(i0, count):
        return dot(slots, select[i0 : i0 + count, :], NT)

    for p in range(3):
        i0 = 2 * p * per
        g = ordered(i0, 2 * per)
        lane = lax.broadcasted_iota(jnp.int32, g.shape, 1)
        line = lax.broadcasted_iota(jnp.int32, g.shape, 0)
        g = jnp.where((lane >= per) & (line >= rows), -g, g).astype(BF16)
        cc = dot(g, cos_ref[i0 : i0 + 2 * per, :], NN)
        ss = dot(g, sin_ref[i0 : i0 + 2 * per, :], NN)
        w_ref[2 * p] = cc[:rows] - ss[rows:]
        w_ref[2 * p + 1] = ss[:rows] + cc[rows:]
    for p in range(2):
        i0 = (6 + p) * per
        g = ordered(i0, per).astype(BF16)
        w_ref[6 + p] = dot(g[:rows], cos_ref[i0 : i0 + per, :], NN) - dot(g[rows:], sin_ref[i0 : i0 + per, :], NN)

    tile = 16
    width = 256

    def spread_rows(step, carry):
        r0 = pl.multiple_of(step * tile, tile)
        for x0 in range(0, span, width):
            p1, q1, p2, q2, p3, q3, p0, p4 = (w_ref[n, pl.ds(r0, tile), x0 : x0 + width] for n in range(8))
            e0 = p0 + p4
            e1 = p0 - p4
            plus = e0 + p2
            minus = e0 - p2
            low = e1 - q2
            high = e1 + q2
            t0 = p1 + p3
            t2 = q3 - q1
            t1 = HALF_ROOT * ((p1 - q1) - (p3 + q3))
            t3 = HALF_ROOT * ((p3 - q3) - (p1 + q1))
            pieces = (plus + t0, low + t1, minus + t2, high + t3, plus - t0, low - t1, minus - t2, high - t3)
            for b, piece in enumerate(pieces):
                out_ref[pl.ds(r0, tile), b * span + x0 : b * span + x0 + width] = piece.astype(BF16)
        return carry

    lax.fori_loop(0, rows // tile, spread_rows, 0)


def vmem():
    return pl.BlockSpec(memory_space=pltpu.VMEM)


def smem():
    return pl.BlockSpec(memory_space=pltpu.SMEM)


def call(body, name, outs, specs, scratch):
    return pl.pallas_call(
        body,
        name=name,
        out_shape=outs,
        in_specs=specs,
        out_specs=jax.tree.map(lambda _: vmem(), outs),
        scratch_shapes=scratch,
    )


def on_device(fields, legendre, damping, assignment, truncation):
    field_count, lat_rows, lon_count = fields.shape
    wave_slots, _, pair_slots, half_lat = legendre.shape
    total_waves = assignment.shape[0]
    lat_devices = lax.axis_size("lat")
    fld_devices = lax.axis_size("fld")
    field_total = damping.shape[0]
    rows = field_count * lat_rows
    columns = 2 * field_total
    pairs = 2 * wave_slots
    top = total_waves + 2 * pair_slots * fld_devices - 1
    span = lon_count // RADIX
    block = total_waves * 2 * rows // 128
    cos_table, sin_table = wave_tables(total_waves, lon_count)
    assign_row = assignment.reshape(1, total_waves)

    sent = call(
        forward_kernel, "forward", jax.ShapeDtypeStruct((total_waves, 2 * rows), BF16), [vmem()] * 4,
        [pltpu.VMEM((RADIX, rows, span), BF16)],
    )(fields.reshape(rows, lon_count), assign_row, cos_table, sin_table)
    received = lax.all_to_all(sent.reshape(lat_devices, wave_slots, 2 * rows), "lat", 0, 0, tiled=True)
    copies = call(
        fold_kernel, "fold", jax.ShapeDtypeStruct((fld_devices, block, 128), BF16), [vmem()],
        [pltpu.VMEM((total_waves, 2 * rows), F32)],
    )(received.reshape(total_waves, 2 * rows))
    gathered = lax.all_to_all(copies, "fld", 0, 0, tiled=True)
    spectra, partial = call(
        lambda *refs: legendre_kernel(*refs, top=top), "legendre",
        (
            jax.ShapeDtypeStruct((pairs, columns, pair_slots), BF16),
            jax.ShapeDtypeStruct((fld_devices * block, 128), BF16),
        ),
        [vmem(), vmem(), smem(), smem(), smem()],
        [pltpu.VMEM((fld_devices * block, 128), F32), pltpu.VMEM((fld_devices * block, 128), F32)],
    )(
        gathered.reshape(fld_devices * block, 128),
        legendre.reshape(pairs, pair_slots, half_lat),
        damping,
        assignment,
        truncation,
    )
    parts = lax.all_to_all(partial.reshape(fld_devices, block, 128), "fld", 0, 0, tiled=True)
    outgoing = call(
        unfold_kernel, "unfold", jax.ShapeDtypeStruct((total_waves, 2 * rows), BF16), [vmem()],
        [pltpu.VMEM((total_waves, 2 * rows), F32)],
    )(parts)
    returned = lax.all_to_all(outgoing.reshape(lat_devices, wave_slots, 2 * rows), "lat", 0, 0, tiled=True)
    field_out = call(
        inverse_kernel, "inverse", jax.ShapeDtypeStruct((rows, lon_count), BF16), [vmem()] * 4,
        [pltpu.VMEM((RADIX, rows, span), F32)],
    )(returned.reshape(total_waves, 2 * rows), assign_row, cos_table, sin_table)
    return (
        field_out.reshape(field_count, lat_rows, lon_count),
        spectra.reshape(wave_slots, 2, field_total, 2, pair_slots),
    )


def solution(mesh):
    placed = (P("fld", "lat", None), P("lat", None, "fld", None), P(), P(), P())
    return jax.shard_map(
        on_device,
        mesh=mesh,
        in_specs=placed,
        out_specs=(P("fld", "lat", None), P("lat", None, None, None, "fld")),
        check_vma=False,
    )
```

```python
import math

import jax
import jax.numpy as jnp
import numpy as np
from jax import lax
from jax.experimental import pallas as pl
from jax.experimental.pallas import tpu as pltpu
from jax.sharding import PartitionSpec as P

F32 = jnp.float32
BF16 = jnp.bfloat16
RADIX = 8
HALF_ROOT = math.sqrt(0.5)
NT = (((1,), (1,)), ((), ()))
NN = (((1,), (0,)), ((), ()))
CLASS_ORDER = (1, 7, 2, 6, 3, 5, 8, 4)


def dot(a, b, dims):
    return lax.dot_general(a, b, dims, preferred_element_type=F32)


def wave_tables(total_waves, lon_count):
    span = lon_count // RADIX
    per = total_waves // RADIX
    waves = np.concatenate([RADIX * np.arange(per) + c for c in CLASS_ORDER])
    phase = (waves[:, None] * np.arange(span)[None, :]) % lon_count
    angle = phase * (2.0 * np.pi / lon_count)
    sign = np.repeat([1.0, -1.0, 1.0, -1.0, 1.0, -1.0, 1.0, 1.0], per)[:, None]
    factor = math.sqrt(2.0 / lon_count)
    return (
        jnp.asarray((factor * np.cos(angle)).astype(np.float32), BF16),
        jnp.asarray((factor * sign * np.sin(angle)).astype(np.float32), BF16),
    )


def wave_select(assign_row, total_waves):
    per = total_waves // RADIX
    row = lax.broadcasted_iota(jnp.int32, (total_waves, total_waves), 0)
    block = row // per
    cls = jnp.full_like(row, CLASS_ORDER[0])
    for b in range(1, RADIX):
        cls = jnp.where(block == b, CLASS_ORDER[b], cls)
    wave = RADIX * (row % per) + cls - 1
    return jnp.where(wave == assign_row, 1.0, 0.0).astype(BF16)


def forward_kernel(
    fields_hbm, assign_hbm, cos_hbm, sin_hbm, table_hbm,
    out_ref, assign_ref, cos_ref, sin_ref, table_ref, fields_ref, z_ref, sems,
):
    rows, lon_count = fields_ref.shape
    waves, span = cos_ref.shape
    per = waves // RADIX
    tile = 16
    width = 256
    steps = rows // tile

    def rows_copy(step):
        at = pl.ds(pl.multiple_of(step * tile, tile), tile)
        return pltpu.make_async_copy(fields_hbm.at[at], fields_ref.at[at], sems.at[step])

    for step in range(steps):
        rows_copy(step).start()
    moves = ((assign_hbm, assign_ref), (cos_hbm, cos_ref), (sin_hbm, sin_ref), (table_hbm, table_ref))
    loads = [pltpu.make_async_copy(*move, sems.at[steps + n]) for n, move in enumerate(moves)]
    for load in loads:
        load.start()

    def fold_rows(step, carry):
        r0 = pl.multiple_of(step * tile, tile)
        rows_copy(step).wait()
        for x0 in range(0, span, width):
            s = []
            for b in range(RADIX):
                v = fields_ref[pl.ds(r0, tile), b * span + x0 : b * span + x0 + width].astype(F32)
                s.append(v * v)
            e = [s[b] + s[b + 4] for b in range(4)]
            o = [s[b] - s[b + 4] for b in range(4)]
            u = HALF_ROOT * (o[1] - o[3])
            v = HALF_ROOT * (o[1] + o[3])
            even = e[0] + e[2]
            odd = e[1] + e[3]
            parts = (
                o[0] + u, -(o[2] + v),
                e[0] - e[2], e[3] - e[1],
                o[0] - u, o[2] - v,
                even + odd, even - odd,
            )
            for n, part in enumerate(parts):
                z_ref[n, pl.ds(r0, tile), x0 : x0 + width] = part.astype(BF16)
        return carry

    lax.fori_loop(0, steps, fold_rows, 0)
    for load in loads[:3]:
        load.wait()
    select = wave_select(assign_ref[...], waves)
    acc = jnp.zeros((2 * rows, waves), F32)
    for p in range(3):
        i0 = 2 * p * per
        zz = z_ref[2 * p : 2 * p + 2].reshape(2 * rows, span)
        dc = dot(zz, cos_ref[i0 : i0 + 2 * per, :], NT)
        ds = dot(zz, sin_ref[i0 : i0 + 2 * per, :], NT)
        real = dc[:rows] + ds[rows:]
        imag = dc[rows:] - ds[:rows]
        lane = lax.broadcasted_iota(jnp.int32, imag.shape, 1)
        imag = jnp.where(lane < per, imag, -imag)
        both = jnp.concatenate([real, imag], axis=0).astype(BF16)
        acc = acc + dot(both, select[i0 : i0 + 2 * per, :], NN)
    for p in range(2):
        i0 = (6 + p) * per
        z = z_ref[6 + p]
        real = dot(z, cos_ref[i0 : i0 + per, :], NT)
        imag = -dot(z, sin_ref[i0 : i0 + per, :], NT)
        both = jnp.concatenate([real, imag], axis=0).astype(BF16)
        acc = acc + dot(both, select[i0 : i0 + per, :], NN)
    out_ref[...] = acc.T.astype(BF16)
    loads[3].wait()


def fold_kernel(in_ref, out_ref, x_ref):
    copies = out_ref.shape[0]
    total = in_ref.shape[0]
    slots = 4
    half = total // 2
    x_ref[...] = in_ref[...].astype(F32)
    block = lax.broadcasted_iota(jnp.int32, (8, 128), 1) // 32
    for s in range(slots):
        folded = ([], [])
        for part in range(4):
            north = x_ref[pl.ds(4 * part + s, 8, stride=16), :]
            south = x_ref[pl.ds(half + 4 * part + s, 8, stride=16), :]
            folded[0].append((north + south) * 0.5)
            folded[1].append((north - south) * 0.5)
        for f in range(2):
            for r in range(2):
                source = 2 * r + f
                pair = []
                for a in range(2):
                    rows = None
                    for part in range(4):
                        shift = (32 * (part - source)) % 128
                        moved = folded[a][part]
                        if shift:
                            moved = pltpu.roll(moved, shift, 1)
                        rows = moved if rows is None else jnp.where(block == part, moved, rows)
                    pair.append(rows)
                tile = jnp.concatenate(pair, axis=0).astype(BF16)
                row = ((2 * f + r) * 8 + 2 * s) * 8
                for copy in range(copies):
                    out_ref[copy, row : row + 16, :] = tile


def legendre_kernel(x_ref, table_ref, damping_ref, assign_ref, limit_ref, spectra_ref, out_ref, wide_ref, sums_ref, *, top):
    pairs, degrees, half_lat = table_ref.shape
    columns = spectra_ref.shape[1]
    slots = pairs // 2
    groups = half_lat // 128
    stride = pairs * groups
    slot0 = lax.axis_index("lat") * slots
    first = lax.axis_index("fld") * degrees
    wide_ref[...] = x_ref[...].astype(F32)
    field = lax.broadcasted_iota(jnp.int32, (columns, degrees), 0) // 2
    damp = jnp.zeros((columns, degrees), F32)
    for n in range(columns // 2):
        damp = jnp.where(field == n, damping_ref[n], damp)
    pair_index = first + lax.broadcasted_iota(jnp.int32, (columns, degrees), 1)
    for s in range(slots):
        wave = assign_ref[slot0 + s]
        limit = limit_ref[wave]
        for a in range(2):
            sa = 2 * s + a
            rows = jnp.concatenate(
                [wide_ref[pl.ds(sa * groups + g, columns, stride=stride), :] for g in range(groups)], axis=1
            ).astype(BF16)
            table = table_ref[sa]
            coefficient = dot(rows, table, NT)
            offset = 2 * pair_index + a
            degree = (wave + 1 + offset).astype(F32)
            ratio = degree * (degree + 1.0) / float(top * (top + 1))
            scaled = coefficient / (1.0 + damp * (ratio * ratio))
            diffused = jnp.where(offset < limit, scaled, 0.0).astype(BF16)
            spectra_ref[sa] = diffused
            back = dot(diffused, table, NN)
            for g in range(groups):
                sums_ref[pl.ds(sa * groups + g, columns, stride=stride), :] = back[:, g * 128 : g * 128 + 128]
    out_ref[...] = sums_ref[...].astype(BF16)


def unfold_kernel(in_ref, out_ref, y_ref):
    sources, total, _ = in_ref.shape
    half = total // 2
    block = lax.broadcasted_iota(jnp.int32, (8, 128), 1) // 32

    def summed(row):
        acc = in_ref[0, row : row + 16, :].astype(F32)
        for n in range(1, sources):
            acc = acc + in_ref[n, row : row + 16, :].astype(F32)
        return acc.astype(BF16).astype(F32)

    for s in range(4):
        north, south = {}, {}
        for f in range(2):
            for r in range(2):
                both = summed(((2 * f + r) * 8 + 2 * s) * 8)
                north[2 * r + f] = both[:8] + both[8:]
                south[2 * r + f] = both[:8] - both[8:]
        for part in range(4):
            for base, rows_of in ((0, north), (half, south)):
                rows = None
                for target in range(4):
                    shift = (32 * (target - part)) % 128
                    moved = rows_of[target]
                    if shift:
                        moved = pltpu.roll(moved, shift, 1)
                    rows = moved if rows is None else jnp.where(block == target, moved, rows)
                y_ref[pl.ds(base + 4 * part + s, 8, stride=16), :] = rows
    out_ref[...] = y_ref[...].astype(BF16)


def inverse_kernel(in_ref, assign_ref, cos_ref, sin_ref, out_hbm, w_ref, out_ref, sems):
    rows, lon_count = out_ref.shape
    waves, span = cos_ref.shape
    per = waves // RADIX
    select = wave_select(assign_ref[...], waves)
    slots = in_ref[...].astype(F32).T.astype(BF16)

    def ordered(i0, count):
        return dot(slots, select[i0 : i0 + count, :], NT)

    for p in range(3):
        i0 = 2 * p * per
        g = ordered(i0, 2 * per)
        lane = lax.broadcasted_iota(jnp.int32, g.shape, 1)
        line = lax.broadcasted_iota(jnp.int32, g.shape, 0)
        g = jnp.where((lane >= per) & (line >= rows), -g, g).astype(BF16)
        cc = dot(g, cos_ref[i0 : i0 + 2 * per, :], NN)
        ss = dot(g, sin_ref[i0 : i0 + 2 * per, :], NN)
        w_ref[2 * p] = cc[:rows] - ss[rows:]
        w_ref[2 * p + 1] = ss[:rows] + cc[rows:]
    for p in range(2):
        i0 = (6 + p) * per
        g = ordered(i0, per).astype(BF16)
        w_ref[6 + p] = dot(g[:rows], cos_ref[i0 : i0 + per, :], NN) - dot(g[rows:], sin_ref[i0 : i0 + per, :], NN)

    tile = 16
    width = 256

    def rows_copy(step):
        at = pl.ds(pl.multiple_of(step * tile, tile), tile)
        return pltpu.make_async_copy(out_ref.at[at], out_hbm.at[at], sems.at[step])

    def spread_rows(step, carry):
        r0 = pl.multiple_of(step * tile, tile)
        for x0 in range(0, span, width):
            p1, q1, p2, q2, p3, q3, p0, p4 = (w_ref[n, pl.ds(r0, tile), x0 : x0 + width] for n in range(8))
            e0 = p0 + p4
            e1 = p0 - p4
            plus = e0 + p2
            minus = e0 - p2
            low = e1 - q2
            high = e1 + q2
            t0 = p1 + p3
            t2 = q3 - q1
            t1 = HALF_ROOT * ((p1 - q1) - (p3 + q3))
            t3 = HALF_ROOT * ((p3 - q3) - (p1 + q1))
            pieces = (plus + t0, low + t1, minus + t2, high + t3, plus - t0, low - t1, minus - t2, high - t3)
            for b, piece in enumerate(pieces):
                out_ref[pl.ds(r0, tile), b * span + x0 : b * span + x0 + width] = piece.astype(BF16)
        rows_copy(step).start()
        return carry

    lax.fori_loop(0, rows // tile, spread_rows, 0)
    for step in range(rows // tile):
        rows_copy(step).wait()


VMEM = pl.BlockSpec(memory_space=pltpu.VMEM)
SMEM = pl.BlockSpec(memory_space=pltpu.SMEM)
HBM = pl.BlockSpec(memory_space=pltpu.HBM)


def in_vmem(array):
    return pltpu.with_memory_space_constraint(array, pltpu.VMEM)


def in_hbm(array):
    return pltpu.with_memory_space_constraint(array, pltpu.HBM)


def call(body, name, outs, specs, scratch, out_specs=None):
    if out_specs is None:
        out_specs = tuple(VMEM for _ in outs)
    return pl.pallas_call(
        body,
        name=name,
        out_shape=outs,
        in_specs=specs,
        out_specs=out_specs,
        scratch_shapes=scratch,
        compiler_params=pltpu.CompilerParams(vmem_limit_bytes=16 << 20),
    )


def on_device(fields, legendre, damping, assignment, truncation):
    field_count, lat_rows, lon_count = fields.shape
    wave_slots, _, pair_slots, half_lat = legendre.shape
    total_waves = assignment.shape[0]
    lat_devices = lax.axis_size("lat")
    fld_devices = lax.axis_size("fld")
    field_total = damping.shape[0]
    rows = field_count * lat_rows
    columns = 2 * field_total
    pairs = 2 * wave_slots
    top = total_waves + 2 * pair_slots * fld_devices - 1
    span = lon_count // RADIX
    steps = rows // 16
    block = total_waves * 2 * rows // 128
    by_wave = pltpu.VMEM((total_waves, 2 * rows), BF16)
    wide = pltpu.VMEM((total_waves, 2 * rows), F32)
    gathered_wide = pltpu.VMEM((fld_devices * block, 128), F32)

    sent, assign_row, cos_table, sin_table, table = call(
        forward_kernel, "forward",
        (
            by_wave,
            pltpu.VMEM((1, total_waves), jnp.int32),
            pltpu.VMEM((total_waves, span), BF16),
            pltpu.VMEM((total_waves, span), BF16),
            pltpu.VMEM((pairs, pair_slots, half_lat), BF16),
        ),
        [HBM] * 5,
        [
            pltpu.VMEM((rows, lon_count), BF16),
            pltpu.VMEM((RADIX, rows, span), BF16),
            pltpu.SemaphoreType.DMA((steps + 4,)),
        ],
    )(
        in_hbm(fields.reshape(rows, lon_count)),
        in_hbm(assignment.reshape(1, total_waves)),
        *map(in_hbm, wave_tables(total_waves, lon_count)),
        in_hbm(legendre.reshape(pairs, pair_slots, half_lat)),
    )
    received = lax.all_to_all(sent.reshape(lat_devices, wave_slots, 2 * rows), "lat", 0, 0, tiled=True)
    (copies,) = call(
        fold_kernel, "fold", (pltpu.VMEM((fld_devices, block, 128), BF16),), [VMEM], [wide]
    )(in_vmem(received.reshape(total_waves, 2 * rows)))
    gathered = lax.all_to_all(copies, "fld", 0, 0, tiled=True)
    spectra, partial = call(
        lambda *refs: legendre_kernel(*refs, top=top), "legendre",
        (
            jax.ShapeDtypeStruct((pairs, columns, pair_slots), BF16),
            pltpu.VMEM((fld_devices * block, 128), BF16),
        ),
        [VMEM, VMEM, SMEM, SMEM, SMEM],
        [gathered_wide, gathered_wide],
    )(in_vmem(gathered.reshape(fld_devices * block, 128)), in_vmem(table), damping, assignment, truncation)
    parts = lax.all_to_all(partial.reshape(fld_devices, block, 128), "fld", 0, 0, tiled=True)
    (outgoing,) = call(unfold_kernel, "unfold", (by_wave,), [VMEM], [wide])(in_vmem(parts))
    returned = lax.all_to_all(outgoing.reshape(lat_devices, wave_slots, 2 * rows), "lat", 0, 0, tiled=True)
    (field_out,) = call(
        inverse_kernel, "inverse", (jax.ShapeDtypeStruct((rows, lon_count), BF16),), [VMEM] * 4,
        [
            pltpu.VMEM((RADIX, rows, span), F32),
            pltpu.VMEM((rows, lon_count), BF16),
            pltpu.SemaphoreType.DMA((steps,)),
        ],
        (HBM,),
    )(in_vmem(returned.reshape(total_waves, 2 * rows)), in_vmem(assign_row), in_vmem(cos_table), in_vmem(sin_table))
    return (
        field_out.reshape(field_count, lat_rows, lon_count),
        spectra.reshape(wave_slots, 2, field_total, 2, pair_slots),
    )


def solution(mesh):
    placed = (P("fld", "lat", None), P("lat", None, "fld", None), P(), P(), P())
    return jax.shard_map(
        on_device,
        mesh=mesh,
        in_specs=placed,
        out_specs=(P("fld", "lat", None), P("lat", None, None, None, "fld")),
        check_vma=False,
    )
```

```python
import math

import jax
import jax.numpy as jnp
import numpy as np
from jax import lax
from jax.experimental import pallas as pl
from jax.experimental.pallas import tpu as pltpu
from jax.sharding import PartitionSpec as P

F32 = jnp.float32
BF16 = jnp.bfloat16
RADIX = 8
HALF_ROOT = math.sqrt(0.5)
NT = (((1,), (1,)), ((), ()))
NN = (((1,), (0,)), ((), ()))
CLASS_ORDER = (1, 7, 2, 6, 3, 5, 8, 4)


def dot(a, b, dims):
    return lax.dot_general(a, b, dims, preferred_element_type=F32)


def wave_table(total_waves, lon_count):
    span = lon_count // RADIX
    per = total_waves // RADIX
    factor = math.sqrt(2.0 / lon_count)
    blocks = []
    for classes in ((1, 7), (2, 6), (3, 5), (8,), (4,)):
        waves = np.concatenate([RADIX * np.arange(per) + c for c in classes])
        angle = (waves[:, None] * np.arange(span)[None, :] % lon_count) * (2.0 * np.pi / lon_count)
        sign = np.where(np.arange(len(waves)) < per, 1.0, -1.0)[:, None]
        blocks += [factor * np.cos(angle), factor * sign * np.sin(angle)]
    return jnp.asarray(np.concatenate(blocks).astype(np.float32), BF16)


def forward_kernel(
    fields_hbm, assign_hbm, trig_hbm, table_hbm, damping_hbm, limit_hbm,
    out_ref, select_ref, trig_ref, table_ref, scale_ref,
    fields_ref, z_ref, assign_ref, damping_ref, slot_ref, limit_ref, sems, *, top,
):
    rows, lon_count = fields_ref.shape
    waves = select_ref.shape[0]
    span = trig_ref.shape[1]
    per = waves // RADIX
    tile = 16
    width = 256
    steps = rows // tile

    def rows_copy(step):
        at = pl.ds(pl.multiple_of(step * tile, tile), tile)
        return pltpu.make_async_copy(fields_hbm.at[at], fields_ref.at[at], sems.at[step])

    moves = (
        (damping_hbm, damping_ref), (assign_hbm, slot_ref), (limit_hbm, limit_ref), (assign_hbm, assign_ref),
        (trig_hbm, trig_ref), (table_hbm, table_ref),
    )
    loads = [pltpu.make_async_copy(*move, sems.at[steps + n]) for n, move in enumerate(moves)]
    for load in loads[:4]:
        load.start()
    for step in range(steps):
        rows_copy(step).start()
    loads[4].start()
    for load in loads[:4]:
        load.wait()

    pairs, columns, degrees = scale_ref.shape
    slots = pairs // 2
    slot0 = lax.axis_index("lat") * slots
    first = lax.axis_index("fld") * degrees
    field = lax.broadcasted_iota(jnp.int32, (columns, degrees), 0) // 2
    damp = jnp.zeros((columns, degrees), F32)
    for n in range(columns // 2):
        damp = jnp.where(field == n, damping_ref[0, n], damp)
    pair_index = first + lax.broadcasted_iota(jnp.int32, (8, degrees), 1)
    for s in range(slots):
        wave = slot_ref[0, slot0 + s]
        limit = limit_ref[0, wave]
        for a in range(2):
            offset = 2 * pair_index + a
            degree = (wave + 1 + offset).astype(F32)
            ratio = degree * (degree + 1.0) / float(top * (top + 1))
            square = ratio * ratio
            kept = offset < limit
            for c in range(0, columns, 8):
                factor = 1.0 / (1.0 + damp[c : c + 8] * square)
                scale_ref[2 * s + a, c : c + 8, :] = jnp.where(kept, factor, 0.0)

    wave_of = RADIX * lax.broadcasted_iota(jnp.int32, (per, waves), 0) - 1
    for n, cls in enumerate(CLASS_ORDER):
        hit = (wave_of + cls) == assign_ref[...]
        select_ref[n * per : (n + 1) * per, :] = jnp.where(hit, 1.0, 0.0).astype(BF16)

    loads[5].start()

    def fold_rows(step, carry):
        r0 = pl.multiple_of(step * tile, tile)
        rows_copy(step).wait()
        for x0 in range(0, span, width):
            s = []
            for b in range(RADIX):
                v = fields_ref[pl.ds(r0, tile), b * span + x0 : b * span + x0 + width].astype(F32)
                s.append(v * v)
            e = [s[b] + s[b + 4] for b in range(4)]
            o = [s[b] - s[b + 4] for b in range(4)]
            u = HALF_ROOT * (o[1] - o[3])
            v = HALF_ROOT * (o[1] + o[3])
            even = e[0] + e[2]
            odd = e[1] + e[3]
            parts = (
                o[0] + u, -(o[2] + v),
                e[0] - e[2], e[3] - e[1],
                o[0] - u, o[2] - v,
                even + odd, even - odd,
            )
            for n, part in enumerate(parts):
                z_ref[n, pl.ds(r0, tile), x0 : x0 + width] = part.astype(BF16)
        return carry

    lax.fori_loop(0, steps, fold_rows, 0)
    loads[4].wait()
    acc = jnp.zeros((2 * rows, waves), F32)
    for p in range(3):
        wide = 2 * per
        zz = z_ref[2 * p : 2 * p + 2].reshape(2 * rows, span)
        d = dot(zz, trig_ref[2 * p * wide : 2 * (p + 1) * wide, :], NT)
        turned = pltpu.roll(d, wide, 1)
        real = d[:rows] + turned[rows:]
        imag = d[rows:] - turned[:rows]
        lane = lax.broadcasted_iota(jnp.int32, imag.shape, 1)
        imag = jnp.where((lane & per) == 0, imag, -imag)
        both = jnp.concatenate([real, imag], axis=0).astype(BF16)[:, :wide]
        acc = acc + dot(both, select_ref[p * wide : (p + 1) * wide, :], NN)
    for p in range(2):
        i0 = (6 + p) * per
        d = dot(z_ref[6 + p], trig_ref[2 * i0 : 2 * (i0 + per), :], NT)
        both = jnp.concatenate([d[:, :per], -d[:, per:]], axis=0).astype(BF16)
        acc = acc + dot(both, select_ref[i0 : i0 + per, :], NN)
    out_ref[...] = acc.T.astype(BF16)
    loads[5].wait()


def fold_kernel(in_ref, out_ref, x_ref):
    copies = out_ref.shape[0]
    total = in_ref.shape[0]
    slots = 4
    half = total // 2
    x_ref[...] = in_ref[...].astype(F32)
    block = lax.broadcasted_iota(jnp.int32, (8, 128), 1) // 32
    for s in range(slots):
        folded = ([], [])
        for part in range(4):
            north = x_ref[pl.ds(4 * part + s, 8, stride=16), :]
            south = x_ref[pl.ds(half + 4 * part + s, 8, stride=16), :]
            folded[0].append((north + south) * 0.5)
            folded[1].append((north - south) * 0.5)
        for f in range(2):
            for r in range(2):
                source = 2 * r + f
                pair = []
                for a in range(2):
                    rows = None
                    for part in range(4):
                        shift = (32 * (part - source)) % 128
                        moved = folded[a][part]
                        if shift:
                            moved = pltpu.roll(moved, shift, 1)
                        rows = moved if rows is None else jnp.where(block == part, moved, rows)
                    pair.append(rows)
                tile = jnp.concatenate(pair, axis=0).astype(BF16)
                row = ((2 * f + r) * 8 + 2 * s) * 8
                for copy in range(copies):
                    out_ref[copy, row : row + 16, :] = tile


def legendre_kernel(x_ref, table_ref, scale_ref, spectra_ref, out_ref, wide_ref, sums_ref):
    pairs, degrees, half_lat = table_ref.shape
    columns = spectra_ref.shape[1]
    slots = pairs // 2
    groups = half_lat // 128
    stride = pairs * groups

    def widen(s):
        for n in range(columns):
            at = slice(n * stride + 2 * s * groups, n * stride + 2 * (s + 1) * groups)
            wide_ref[at, :] = x_ref[at, :].astype(F32)

    def narrow(s):
        for n in range(columns):
            at = slice(n * stride + 2 * s * groups, n * stride + 2 * (s + 1) * groups)
            out_ref[at, :] = sums_ref[at, :].astype(BF16)

    def analyse(sa):
        rows = [wide_ref[pl.ds(sa * groups + g, columns, stride=stride), :] for g in range(groups)]
        return dot(jnp.concatenate(rows, axis=1).astype(BF16), table_ref[sa], NT)

    def synthesise(sa, coefficient):
        diffused = (coefficient * scale_ref[sa]).astype(BF16)
        spectra_ref[sa] = diffused
        back = dot(diffused, table_ref[sa], NN)
        for g in range(groups):
            sums_ref[pl.ds(sa * groups + g, columns, stride=stride), :] = back[:, g * 128 : g * 128 + 128]

    widen(0)
    coefficients = [analyse(0), analyse(1)]
    for s in range(slots):
        if s + 1 < slots:
            widen(s + 1)
        for a in range(2):
            if s + 1 < slots:
                coefficients.append(analyse(2 * s + 2 + a))
            synthesise(2 * s + a, coefficients[2 * s + a])
        if s > 0:
            narrow(s - 1)
    narrow(slots - 1)


def unfold_kernel(in_ref, out_ref, y_ref):
    sources, total, _ = in_ref.shape
    half = total // 2
    block = lax.broadcasted_iota(jnp.int32, (8, 128), 1) // 32

    def summed(row):
        acc = in_ref[0, row : row + 16, :].astype(F32)
        for n in range(1, sources):
            acc = acc + in_ref[n, row : row + 16, :].astype(F32)
        return acc.astype(BF16).astype(F32)

    for s in range(4):
        north, south = {}, {}
        for f in range(2):
            for r in range(2):
                both = summed(((2 * f + r) * 8 + 2 * s) * 8)
                north[2 * r + f] = both[:8] + both[8:]
                south[2 * r + f] = both[:8] - both[8:]
        for part in range(4):
            for base, rows_of in ((0, north), (half, south)):
                rows = None
                for target in range(4):
                    shift = (32 * (target - part)) % 128
                    moved = rows_of[target]
                    if shift:
                        moved = pltpu.roll(moved, shift, 1)
                    rows = moved if rows is None else jnp.where(block == target, moved, rows)
                y_ref[pl.ds(base + 4 * part + s, 8, stride=16), :] = rows
    out_ref[...] = y_ref[...].astype(BF16)


def inverse_kernel(in_ref, select_ref, trig_ref, out_hbm, w_ref, out_ref, sems):
    rows, lon_count = out_ref.shape
    waves = select_ref.shape[0]
    span = trig_ref.shape[1]
    per = waves // RADIX
    slots = in_ref[...].astype(F32).T.astype(BF16)

    def ordered(i0, count):
        part = select_ref[i0 : i0 + count, :]
        both = dot(slots, jnp.concatenate([part, part], axis=0), NT)
        lane = lax.broadcasted_iota(jnp.int32, (rows, 2 * count), 1)
        return both[:rows], both[rows:], lane

    for p in range(3):
        wide = 2 * per
        real, imag, lane = ordered(p * wide, wide)
        imag = jnp.where((lane & per) == 0, imag, -imag)
        first = lane < wide
        g = jnp.concatenate([jnp.where(first, real, -imag), jnp.where(first, imag, real)], axis=0).astype(BF16)
        w = dot(g, trig_ref[2 * p * wide : 2 * (p + 1) * wide, :], NN)
        w_ref[2 * p] = w[:rows]
        w_ref[2 * p + 1] = w[rows:]
    for p in range(2):
        i0 = (6 + p) * per
        real, imag, lane = ordered(i0, per)
        g = jnp.where(lane < per, real, -imag).astype(BF16)
        w_ref[6 + p] = dot(g, trig_ref[2 * i0 : 2 * (i0 + per), :], NN)

    tile = 16
    width = 256

    def rows_copy(step):
        at = pl.ds(pl.multiple_of(step * tile, tile), tile)
        return pltpu.make_async_copy(out_ref.at[at], out_hbm.at[at], sems.at[step])

    def spread_rows(step, carry):
        r0 = pl.multiple_of(step * tile, tile)
        for x0 in range(0, span, width):
            p1, q1, p2, q2, p3, q3, p0, p4 = (w_ref[n, pl.ds(r0, tile), x0 : x0 + width] for n in range(8))
            e0 = p0 + p4
            e1 = p0 - p4
            plus = e0 + p2
            minus = e0 - p2
            low = e1 - q2
            high = e1 + q2
            t0 = p1 + p3
            t2 = q3 - q1
            t1 = HALF_ROOT * ((p1 - q1) - (p3 + q3))
            t3 = HALF_ROOT * ((p3 - q3) - (p1 + q1))
            pieces = (plus + t0, low + t1, minus + t2, high + t3, plus - t0, low - t1, minus - t2, high - t3)
            for b, piece in enumerate(pieces):
                out_ref[pl.ds(r0, tile), b * span + x0 : b * span + x0 + width] = piece.astype(BF16)
        rows_copy(step).start()
        return carry

    lax.fori_loop(0, rows // tile, spread_rows, 0)
    for step in range(rows // tile):
        rows_copy(step).wait()


VMEM = pl.BlockSpec(memory_space=pltpu.VMEM)
HBM = pl.BlockSpec(memory_space=pltpu.HBM)


def in_vmem(array):
    return pltpu.with_memory_space_constraint(array, pltpu.VMEM)


def in_hbm(array):
    return pltpu.with_memory_space_constraint(array, pltpu.HBM)


def call(body, name, outs, specs, scratch, out_specs=None):
    if out_specs is None:
        out_specs = tuple(VMEM for _ in outs)
    return pl.pallas_call(
        body,
        name=name,
        out_shape=outs,
        in_specs=specs,
        out_specs=out_specs,
        scratch_shapes=scratch,
        compiler_params=pltpu.CompilerParams(vmem_limit_bytes=16 << 20),
    )


def on_device(fields, legendre, damping, assignment, truncation):
    field_count, lat_rows, lon_count = fields.shape
    wave_slots, _, pair_slots, half_lat = legendre.shape
    total_waves = assignment.shape[0]
    lat_devices = lax.axis_size("lat")
    fld_devices = lax.axis_size("fld")
    field_total = damping.shape[0]
    rows = field_count * lat_rows
    columns = 2 * field_total
    pairs = 2 * wave_slots
    top = total_waves + 2 * pair_slots * fld_devices - 1
    span = lon_count // RADIX
    steps = rows // 16
    block = total_waves * 2 * rows // 128
    by_wave = pltpu.VMEM((total_waves, 2 * rows), BF16)
    wide = pltpu.VMEM((total_waves, 2 * rows), F32)
    gathered_wide = pltpu.VMEM((fld_devices * block, 128), F32)

    scalars = lambda array: in_hbm(array.reshape(1, array.shape[0]))
    sent, select, trig, table, scale = call(
        lambda *refs: forward_kernel(*refs, top=top), "forward",
        (
            by_wave,
            pltpu.VMEM((total_waves, total_waves), BF16),
            pltpu.VMEM((2 * total_waves, span), BF16),
            pltpu.VMEM((pairs, pair_slots, half_lat), BF16),
            pltpu.VMEM((pairs, columns, pair_slots), F32),
        ),
        [HBM] * 6,
        [
            pltpu.VMEM((rows, lon_count), BF16),
            pltpu.VMEM((RADIX, rows, span), BF16),
            pltpu.VMEM((1, total_waves), jnp.int32),
            pltpu.SMEM((1, field_total), F32),
            pltpu.SMEM((1, total_waves), jnp.int32),
            pltpu.SMEM((1, total_waves), jnp.int32),
            pltpu.SemaphoreType.DMA((steps + 6,)),
        ],
    )(
        in_hbm(fields.reshape(rows, lon_count)),
        scalars(assignment),
        in_hbm(wave_table(total_waves, lon_count)),
        in_hbm(legendre.reshape(pairs, pair_slots, half_lat)),
        scalars(damping),
        scalars(truncation),
    )
    received = lax.all_to_all(sent.reshape(lat_devices, wave_slots, 2 * rows), "lat", 0, 0, tiled=True)
    (copies,) = call(
        fold_kernel, "fold", (pltpu.VMEM((fld_devices, block, 128), BF16),), [VMEM], [wide]
    )(in_vmem(received.reshape(total_waves, 2 * rows)))
    gathered = lax.all_to_all(copies, "fld", 0, 0, tiled=True)
    spectra, partial = call(
        legendre_kernel, "legendre",
        (
            jax.ShapeDtypeStruct((pairs, columns, pair_slots), BF16),
            pltpu.VMEM((fld_devices * block, 128), BF16),
        ),
        [VMEM] * 3,
        [gathered_wide, gathered_wide],
    )(in_vmem(gathered.reshape(fld_devices * block, 128)), in_vmem(table), in_vmem(scale))
    parts = lax.all_to_all(partial.reshape(fld_devices, block, 128), "fld", 0, 0, tiled=True)
    (outgoing,) = call(unfold_kernel, "unfold", (by_wave,), [VMEM], [wide])(in_vmem(parts))
    returned = lax.all_to_all(outgoing.reshape(lat_devices, wave_slots, 2 * rows), "lat", 0, 0, tiled=True)
    (field_out,) = call(
        inverse_kernel, "inverse", (jax.ShapeDtypeStruct((rows, lon_count), BF16),), [VMEM] * 3,
        [
            pltpu.VMEM((RADIX, rows, span), F32),
            pltpu.VMEM((rows, lon_count), BF16),
            pltpu.SemaphoreType.DMA((steps,)),
        ],
        (HBM,),
    )(in_vmem(returned.reshape(total_waves, 2 * rows)), in_vmem(select), in_vmem(trig))
    return (
        field_out.reshape(field_count, lat_rows, lon_count),
        spectra.reshape(wave_slots, 2, field_total, 2, pair_slots),
    )


def solution(mesh):
    placed = (P("fld", "lat", None), P("lat", None, "fld", None), P(), P(), P())
    return jax.shard_map(
        on_device,
        mesh=mesh,
        in_specs=placed,
        out_specs=(P("fld", "lat", None), P("lat", None, None, None, "fld")),
        check_vma=False,
    )
```

```python
import math

import jax
import jax.numpy as jnp
import numpy as np
from jax import lax
from jax.experimental import pallas as pl
from jax.experimental.pallas import tpu as pltpu
from jax.sharding import PartitionSpec as P

F32 = jnp.float32
BF16 = jnp.bfloat16
RADIX = 8
HALF_ROOT = math.sqrt(0.5)
NT = (((1,), (1,)), ((), ()))
NN = (((1,), (0,)), ((), ()))
CLASS_ORDER = (1, 7, 2, 6, 3, 5, 8, 4)


def dot(a, b, dims):
    return lax.dot_general(a, b, dims, preferred_element_type=F32)


def wave_table(total_waves, lon_count):
    span = lon_count // RADIX
    per = total_waves // RADIX
    factor = math.sqrt(2.0 / lon_count)
    blocks = []
    for classes in ((1, 7), (2, 6), (3, 5), (8,), (4,)):
        waves = np.concatenate([RADIX * np.arange(per) + c for c in classes])
        angle = (waves[:, None] * np.arange(span)[None, :] % lon_count) * (2.0 * np.pi / lon_count)
        sign = np.where(np.arange(len(waves)) < per, 1.0, -1.0)[:, None]
        blocks += [factor * np.cos(angle), factor * sign * np.sin(angle)]
    return jnp.asarray(np.concatenate(blocks).astype(np.float32), BF16)


def forward_kernel(
    fields_hbm, assign_hbm, trig_hbm, table_hbm, damping_hbm, limit_hbm,
    out_ref, select_ref, trig_ref, table_ref, scale_ref,
    fields_ref, z_ref, assign_ref, damping_ref, slot_ref, limit_ref, sems, *, top,
):
    rows, lon_count = fields_ref.shape
    waves = select_ref.shape[0]
    span = trig_ref.shape[1]
    per = waves // RADIX
    tile = 16
    width = 256
    steps = rows // tile

    def rows_copy(step):
        at = pl.ds(pl.multiple_of(step * tile, tile), tile)
        return pltpu.make_async_copy(fields_hbm.at[at], fields_ref.at[at], sems.at[step])

    moves = (
        (damping_hbm, damping_ref), (assign_hbm, slot_ref), (limit_hbm, limit_ref), (assign_hbm, assign_ref),
        (trig_hbm, trig_ref), (table_hbm, table_ref),
    )
    loads = [pltpu.make_async_copy(*move, sems.at[steps + n]) for n, move in enumerate(moves)]
    for load in loads[:4]:
        load.start()
    for step in range(steps):
        rows_copy(step).start()
    loads[4].start()
    for load in loads[:4]:
        load.wait()

    pairs, columns, degrees = scale_ref.shape
    slots = pairs // 2
    slot0 = lax.axis_index("lat") * slots
    first = lax.axis_index("fld") * degrees
    field = lax.broadcasted_iota(jnp.int32, (columns, degrees), 0) // 2
    damp = jnp.zeros((columns, degrees), F32)
    for n in range(columns // 2):
        damp = jnp.where(field == n, damping_ref[0, n], damp)
    pair_index = first + lax.broadcasted_iota(jnp.int32, (8, degrees), 1)
    for s in range(slots):
        wave = slot_ref[0, slot0 + s]
        limit = limit_ref[0, wave]
        for a in range(2):
            offset = 2 * pair_index + a
            degree = (wave + 1 + offset).astype(F32)
            ratio = degree * (degree + 1.0) / float(top * (top + 1))
            square = ratio * ratio
            kept = offset < limit
            for c in range(0, columns, 8):
                factor = 1.0 / (1.0 + damp[c : c + 8] * square)
                scale_ref[2 * s + a, c : c + 8, :] = jnp.where(kept, factor, 0.0)

    wave_of = RADIX * lax.broadcasted_iota(jnp.int32, (per, waves), 0) - 1
    for n, cls in enumerate(CLASS_ORDER):
        hit = (wave_of + cls) == assign_ref[...]
        select_ref[n * per : (n + 1) * per, :] = jnp.where(hit, 1.0, 0.0).astype(BF16)

    loads[5].start()

    def fold_rows(step, carry):
        r0 = pl.multiple_of(step * tile, tile)
        rows_copy(step).wait()
        for x0 in range(0, span, width):
            s = []
            for b in range(RADIX):
                v = fields_ref[pl.ds(r0, tile), b * span + x0 : b * span + x0 + width].astype(F32)
                s.append(v * v)
            e = [s[b] + s[b + 4] for b in range(4)]
            o = [s[b] - s[b + 4] for b in range(4)]
            u = HALF_ROOT * (o[1] - o[3])
            v = HALF_ROOT * (o[1] + o[3])
            even = e[0] + e[2]
            odd = e[1] + e[3]
            parts = (
                o[0] + u, -(o[2] + v),
                e[0] - e[2], e[3] - e[1],
                o[0] - u, o[2] - v,
                even + odd, even - odd,
            )
            for n, part in enumerate(parts):
                z_ref[n, pl.ds(r0, tile), x0 : x0 + width] = part.astype(BF16)
        return carry

    lax.fori_loop(0, steps, fold_rows, 0)
    loads[4].wait()
    acc = jnp.zeros((2 * rows, waves), F32)
    for p in range(3):
        wide = 2 * per
        zz = z_ref[2 * p : 2 * p + 2].reshape(2 * rows, span)
        d = dot(zz, trig_ref[2 * p * wide : 2 * (p + 1) * wide, :], NT)
        turned = pltpu.roll(d, wide, 1)
        real = d[:rows] + turned[rows:]
        imag = d[rows:] - turned[:rows]
        lane = lax.broadcasted_iota(jnp.int32, imag.shape, 1)
        imag = jnp.where((lane & per) == 0, imag, -imag)
        both = jnp.concatenate([real, imag], axis=0).astype(BF16)[:, :wide]
        acc = acc + dot(both, select_ref[p * wide : (p + 1) * wide, :], NN)
    for p in range(2):
        i0 = (6 + p) * per
        d = dot(z_ref[6 + p], trig_ref[2 * i0 : 2 * (i0 + per), :], NT)
        both = jnp.concatenate([d[:, :per], -d[:, per:]], axis=0).astype(BF16)
        acc = acc + dot(both, select_ref[i0 : i0 + per, :], NN)
    by_slot = acc.T
    upper = lax.broadcasted_iota(jnp.int32, (8, 2 * rows), 0) < 4
    repeats = out_ref.shape[0] // (4 * waves)
    for n in range(waves // 8):
        group = by_slot[8 * n : 8 * n + 8]
        turned = pltpu.roll(group, 4, 0)
        for m, both in enumerate((jnp.where(upper, group, turned), jnp.where(upper, turned, group))):
            both = jnp.concatenate([both, both], axis=0).astype(BF16)
            for k in range(repeats):
                row = ((2 * n + m) * repeats + k) * 16
                out_ref[row : row + 16, :] = both
    loads[5].wait()


def block_transpose(rows):
    block = lax.broadcasted_iota(jnp.int32, rows[0].shape, 1) // 32
    low = block < 2
    even = block % 2 == 0
    half = [None] * 4
    for n in range(2):
        half[n] = jnp.where(low, rows[n], pltpu.roll(rows[n + 2], 64, 1))
        half[n + 2] = jnp.where(low, pltpu.roll(rows[n], 64, 1), rows[n + 2])
    out = [None] * 4
    for n in (0, 2):
        out[n] = jnp.where(even, half[n], pltpu.roll(half[n + 1], 32, 1))
        out[n + 1] = jnp.where(even, pltpu.roll(half[n], 96, 1), half[n + 1])
    return out


def legendre_kernel(x_ref, table_ref, scale_ref, spectra_ref, out_ref, raw_ref, wide_ref, sums_ref, back_ref):
    pairs, degrees, half_lat = table_ref.shape
    columns = spectra_ref.shape[1]
    slots = pairs // 2
    groups = half_lat // 128
    stride = pairs * groups
    owners = columns // 4
    total = x_ref.shape[0]
    half = total // 2
    step = total // 2 // groups
    piece = step // 4
    order = ((0, 0), (0, 1), (1, 0), (1, 1))

    def place(owner, r, f, sa):
        return slice(((4 * owner + 2 * f + r) * pairs + sa) * groups, ((4 * owner + 2 * f + r) * pairs + sa + 1) * groups)

    def fold(s):
        for owner in range(owners):
            folded = ([], [])
            for part in range(4):
                row = part * piece + slots * owner + s
                north = raw_ref[pl.ds(row, groups, stride=step), :]
                south = raw_ref[pl.ds(half + row, groups, stride=step), :]
                folded[0].append((north + south) * 0.5)
                folded[1].append((north - south) * 0.5)
            for a in range(2):
                for (r, f), rows in zip(order, block_transpose(folded[a])):
                    wide_ref[place(owner, r, f, 2 * s + a), :] = rows

    def unfold(s):
        for owner in range(owners):
            north, south = [], []
            for r, f in order:
                even = sums_ref[place(owner, r, f, 2 * s), :]
                odd = sums_ref[place(owner, r, f, 2 * s + 1), :]
                north.append(even + odd)
                south.append(even - odd)
            for base, rows in ((0, north), (half, south)):
                for part, moved in enumerate(block_transpose(rows)):
                    back_ref[pl.ds(base + part * piece + slots * owner + s, groups, stride=step), :] = moved

    def analyse(sa):
        rows = [wide_ref[pl.ds(sa * groups + g, columns, stride=stride), :] for g in range(groups)]
        return dot(jnp.concatenate(rows, axis=1).astype(BF16), table_ref[sa], NT)

    def synthesise(sa, coefficient):
        diffused = (coefficient * scale_ref[sa]).astype(BF16)
        spectra_ref[sa] = diffused
        back = dot(diffused, table_ref[sa], NN)
        for g in range(groups):
            sums_ref[pl.ds(sa * groups + g, columns, stride=stride), :] = back[:, g * 128 : g * 128 + 128]

    raw_ref[...] = x_ref[...].astype(F32)
    fold(0)
    coefficients = [analyse(0), analyse(1)]
    for s in range(slots):
        if s + 1 < slots:
            fold(s + 1)
        for a in range(2):
            if s + 1 < slots:
                coefficients.append(analyse(2 * s + 2 + a))
            synthesise(2 * s + a, coefficients[2 * s + a])
        if s > 0:
            unfold(s - 1)
    unfold(slots - 1)
    out_ref[...] = back_ref[...].astype(BF16)


def inverse_kernel(in_ref, select_ref, trig_ref, out_hbm, w_ref, out_ref, sems):
    rows, lon_count = out_ref.shape
    waves = select_ref.shape[0]
    span = trig_ref.shape[1]
    per = waves // RADIX
    upper = lax.broadcasted_iota(jnp.int32, (8, 2 * rows), 0) < 4
    size = in_ref.shape[0] * 4 // waves

    def summed(n):
        acc = None
        for row in range(n * size, (n + 1) * size, 16):
            both = in_ref[row : row + 16, :].astype(F32)
            both = both[:8] + both[8:]
            acc = both if acc is None else acc + both
        return acc + pltpu.roll(acc, 4, 0)

    slots = [jnp.where(upper, summed(2 * n), summed(2 * n + 1)) for n in range(waves // 8)]
    slots = jnp.concatenate(slots, axis=0).T.astype(BF16)

    def ordered(i0, count):
        part = select_ref[i0 : i0 + count, :]
        both = dot(slots, jnp.concatenate([part, part], axis=0), NT)
        lane = lax.broadcasted_iota(jnp.int32, (rows, 2 * count), 1)
        return both[:rows], both[rows:], lane

    for p in range(3):
        wide = 2 * per
        real, imag, lane = ordered(p * wide, wide)
        imag = jnp.where((lane & per) == 0, imag, -imag)
        first = lane < wide
        g = jnp.concatenate([jnp.where(first, real, -imag), jnp.where(first, imag, real)], axis=0).astype(BF16)
        w = dot(g, trig_ref[2 * p * wide : 2 * (p + 1) * wide, :], NN)
        w_ref[2 * p] = w[:rows]
        w_ref[2 * p + 1] = w[rows:]
    for p in range(2):
        i0 = (6 + p) * per
        real, imag, lane = ordered(i0, per)
        g = jnp.where(lane < per, real, -imag).astype(BF16)
        w_ref[6 + p] = dot(g, trig_ref[2 * i0 : 2 * (i0 + per), :], NN)

    tile = 16
    width = 256

    def rows_copy(step):
        at = pl.ds(pl.multiple_of(step * tile, tile), tile)
        return pltpu.make_async_copy(out_ref.at[at], out_hbm.at[at], sems.at[step])

    def spread_rows(step, carry):
        r0 = pl.multiple_of(step * tile, tile)
        for x0 in range(0, span, width):
            p1, q1, p2, q2, p3, q3, p0, p4 = (w_ref[n, pl.ds(r0, tile), x0 : x0 + width] for n in range(8))
            e0 = p0 + p4
            e1 = p0 - p4
            plus = e0 + p2
            minus = e0 - p2
            low = e1 - q2
            high = e1 + q2
            t0 = p1 + p3
            t2 = q3 - q1
            t1 = HALF_ROOT * ((p1 - q1) - (p3 + q3))
            t3 = HALF_ROOT * ((p3 - q3) - (p1 + q1))
            pieces = (plus + t0, low + t1, minus + t2, high + t3, plus - t0, low - t1, minus - t2, high - t3)
            for b, piece in enumerate(pieces):
                out_ref[pl.ds(r0, tile), b * span + x0 : b * span + x0 + width] = piece.astype(BF16)
        rows_copy(step).start()
        return carry

    lax.fori_loop(0, rows // tile, spread_rows, 0)
    for step in range(rows // tile):
        rows_copy(step).wait()


VMEM = pl.BlockSpec(memory_space=pltpu.VMEM)
HBM = pl.BlockSpec(memory_space=pltpu.HBM)


def in_vmem(array):
    return pltpu.with_memory_space_constraint(array, pltpu.VMEM)


def in_hbm(array):
    return pltpu.with_memory_space_constraint(array, pltpu.HBM)


def call(body, name, outs, specs, scratch, out_specs=None):
    if out_specs is None:
        out_specs = tuple(VMEM for _ in outs)
    return pl.pallas_call(
        body,
        name=name,
        out_shape=outs,
        in_specs=specs,
        out_specs=out_specs,
        scratch_shapes=scratch,
        compiler_params=pltpu.CompilerParams(vmem_limit_bytes=16 << 20),
    )


def on_device(fields, legendre, damping, assignment, truncation):
    field_count, lat_rows, lon_count = fields.shape
    wave_slots, _, pair_slots, half_lat = legendre.shape
    total_waves = assignment.shape[0]
    lat_devices = lax.axis_size("lat")
    fld_devices = lax.axis_size("fld")
    field_total = damping.shape[0]
    rows = field_count * lat_rows
    columns = 2 * field_total
    pairs = 2 * wave_slots
    top = total_waves + 2 * pair_slots * fld_devices - 1
    span = lon_count // RADIX
    steps = rows // 16
    total = fld_devices * total_waves
    message = pltpu.VMEM((total, 2 * rows), BF16)

    def exchange(array):
        array = array.reshape(lat_devices * fld_devices, wave_slots, 2 * rows)
        return in_vmem(lax.all_to_all(array, ("lat", "fld"), 0, 0, tiled=True).reshape(total, 2 * rows))


    scalars = lambda array: in_hbm(array.reshape(1, array.shape[0]))
    sent, select, trig, table, scale = call(
        lambda *refs: forward_kernel(*refs, top=top), "forward",
        (
            message,
            pltpu.VMEM((total_waves, total_waves), BF16),
            pltpu.VMEM((2 * total_waves, span), BF16),
            pltpu.VMEM((pairs, pair_slots, half_lat), BF16),
            pltpu.VMEM((pairs, columns, pair_slots), F32),
        ),
        [HBM] * 6,
        [
            pltpu.VMEM((rows, lon_count), BF16),
            pltpu.VMEM((RADIX, rows, span), BF16),
            pltpu.VMEM((1, total_waves), jnp.int32),
            pltpu.SMEM((1, field_total), F32),
            pltpu.SMEM((1, total_waves), jnp.int32),
            pltpu.SMEM((1, total_waves), jnp.int32),
            pltpu.SemaphoreType.DMA((steps + 6,)),
        ],
    )(
        in_hbm(fields.reshape(rows, lon_count)),
        scalars(assignment),
        in_hbm(wave_table(total_waves, lon_count)),
        in_hbm(legendre.reshape(pairs, pair_slots, half_lat)),
        scalars(damping),
        scalars(truncation),
    )
    spectra, partial = call(
        legendre_kernel, "legendre", (jax.ShapeDtypeStruct((pairs, columns, pair_slots), BF16), message),
        [VMEM] * 3, [pltpu.VMEM((total, 2 * rows), F32)] * 4,
    )(exchange(sent), in_vmem(table), in_vmem(scale))
    (field_out,) = call(
        inverse_kernel, "inverse", (jax.ShapeDtypeStruct((rows, lon_count), BF16),), [VMEM] * 3,
        [
            pltpu.VMEM((RADIX, rows, span), F32),
            pltpu.VMEM((rows, lon_count), BF16),
            pltpu.SemaphoreType.DMA((steps,)),
        ],
        (HBM,),
    )(exchange(partial), in_vmem(select), in_vmem(trig))
    return (
        field_out.reshape(field_count, lat_rows, lon_count),
        spectra.reshape(wave_slots, 2, field_total, 2, pair_slots),
    )


def solution(mesh):
    placed = (P("fld", "lat", None), P("lat", None, "fld", None), P(), P(), P())
    return jax.shard_map(
        on_device,
        mesh=mesh,
        in_specs=placed,
        out_specs=(P("fld", "lat", None), P("lat", None, None, None, "fld")),
        check_vma=False,
    )
```

```python
import math

import jax
import jax.numpy as jnp
import numpy as np
from jax import lax
from jax.experimental import pallas as pl
from jax.experimental.pallas import tpu as pltpu
from jax.sharding import PartitionSpec as P

F32 = jnp.float32
BF16 = jnp.bfloat16
RADIX = 8
HALF_ROOT = math.sqrt(0.5)
NT = (((1,), (1,)), ((), ()))
NN = (((1,), (0,)), ((), ()))
CLASS_ORDER = (1, 7, 2, 6, 3, 5, 8, 4)


def dot(a, b, dims):
    return lax.dot_general(a, b, dims, preferred_element_type=F32)


def wave_table(total_waves, lon_count):
    span = lon_count // RADIX
    per = total_waves // RADIX
    factor = math.sqrt(2.0 / lon_count)
    blocks = []
    for classes in ((1, 7), (2, 6), (3, 5), (8,), (4,)):
        waves = np.concatenate([RADIX * np.arange(per) + c for c in classes])
        angle = (waves[:, None] * np.arange(span)[None, :] % lon_count) * (2.0 * np.pi / lon_count)
        sign = np.where(np.arange(len(waves)) < per, 1.0, -1.0)[:, None]
        blocks += [factor * np.cos(angle), factor * sign * np.sin(angle)]
    return jnp.asarray(np.concatenate(blocks).astype(np.float32), BF16)


def forward_kernel(
    fields_hbm, assign_hbm, trig_hbm, table_hbm, damping_hbm, limit_hbm,
    out_ref, select_ref, trig_ref, table_ref, scale_ref,
    fields_ref, z_ref, assign_ref, damping_ref, slot_ref, limit_ref, sems, *, top,
):
    rows, lon_count = fields_ref.shape
    waves = select_ref.shape[0]
    span = trig_ref.shape[1]
    per = waves // RADIX
    tile = 16
    width = 256
    steps = rows // tile

    def rows_copy(step):
        at = pl.ds(pl.multiple_of(step * tile, tile), tile)
        return pltpu.make_async_copy(fields_hbm.at[at], fields_ref.at[at], sems.at[step])

    moves = (
        (damping_hbm, damping_ref), (assign_hbm, slot_ref), (limit_hbm, limit_ref), (assign_hbm, assign_ref),
        (trig_hbm, trig_ref), (table_hbm, table_ref),
    )
    loads = [pltpu.make_async_copy(*move, sems.at[steps + n]) for n, move in enumerate(moves)]
    for load in loads[:4]:
        load.start()
    for step in range(steps):
        rows_copy(step).start()
    loads[4].start()
    loads[5].start()

    def fold_rows(step, carry):
        r0 = pl.multiple_of(step * tile, tile)
        rows_copy(step).wait()
        for x0 in range(0, span, width):
            s = []
            for b in range(RADIX):
                v = fields_ref[pl.ds(r0, tile), b * span + x0 : b * span + x0 + width].astype(F32)
                s.append(v * v)
            e = [s[b] + s[b + 4] for b in range(4)]
            o = [s[b] - s[b + 4] for b in range(4)]
            u = HALF_ROOT * (o[1] - o[3])
            v = HALF_ROOT * (o[1] + o[3])
            even = e[0] + e[2]
            odd = e[1] + e[3]
            parts = (
                o[0] + u, -(o[2] + v),
                e[0] - e[2], e[3] - e[1],
                o[0] - u, o[2] - v,
                even + odd, even - odd,
            )
            for n, part in enumerate(parts):
                z_ref[n, pl.ds(r0, tile), x0 : x0 + width] = part.astype(BF16)
        return carry

    lax.fori_loop(0, steps, fold_rows, 0)
    for load in loads[:4]:
        load.wait()

    pairs, columns, degrees = scale_ref.shape
    slots = pairs // 2
    slot0 = lax.axis_index("lat") * slots
    first = lax.axis_index("fld") * degrees
    field = lax.broadcasted_iota(jnp.int32, (columns, degrees), 0) // 2
    damp = jnp.zeros((columns, degrees), F32)
    for n in range(columns // 2):
        damp = jnp.where(field == n, damping_ref[0, n], damp)
    pair_index = first + lax.broadcasted_iota(jnp.int32, (8, degrees), 1)
    for s in range(slots):
        wave = slot_ref[0, slot0 + s]
        limit = limit_ref[0, wave]
        for a in range(2):
            offset = 2 * pair_index + a
            degree = (wave + 1 + offset).astype(F32)
            ratio = degree * (degree + 1.0) / float(top * (top + 1))
            square = ratio * ratio
            kept = offset < limit
            for c in range(0, columns, 8):
                factor = 0.5 / (1.0 + damp[c : c + 8] * square)
                scale_ref[2 * s + a, c : c + 8, :] = jnp.where(kept, factor, 0.0)

    wave_of = RADIX * lax.broadcasted_iota(jnp.int32, (per, waves), 0) - 1
    for n, cls in enumerate(CLASS_ORDER):
        hit = (wave_of + cls) == assign_ref[...]
        select_ref[n * per : (n + 1) * per, :] = jnp.where(hit, 1.0, 0.0).astype(BF16)

    loads[4].wait()
    acc = jnp.zeros((2 * rows, waves), F32)
    for p in range(3):
        wide = 2 * per
        zz = z_ref[2 * p : 2 * p + 2].reshape(2 * rows, span)
        d = dot(zz, trig_ref[2 * p * wide : 2 * (p + 1) * wide, :], NT)
        turned = pltpu.roll(d, wide, 1)
        real = d[:rows] + turned[rows:]
        imag = d[rows:] - turned[:rows]
        lane = lax.broadcasted_iota(jnp.int32, imag.shape, 1)
        imag = jnp.where((lane & per) == 0, imag, -imag)
        both = jnp.concatenate([real, imag], axis=0).astype(BF16)[:, :wide]
        acc = acc + dot(both, select_ref[p * wide : (p + 1) * wide, :], NN)
    for p in range(2):
        i0 = (6 + p) * per
        d = dot(z_ref[6 + p], trig_ref[2 * i0 : 2 * (i0 + per), :], NT)
        both = jnp.concatenate([d[:, :per], -d[:, per:]], axis=0).astype(BF16)
        acc = acc + dot(both, select_ref[i0 : i0 + per, :], NN)
    by_slot = acc.T
    upper = lax.broadcasted_iota(jnp.int32, (8, 2 * rows), 0) < 4
    repeats = out_ref.shape[0] // (4 * waves)
    for n in range(waves // 8):
        group = by_slot[8 * n : 8 * n + 8]
        turned = pltpu.roll(group, 4, 0)
        for m, both in enumerate((jnp.where(upper, group, turned), jnp.where(upper, turned, group))):
            both = jnp.concatenate([both, both], axis=0).astype(BF16)
            for k in range(repeats):
                row = ((2 * n + m) * repeats + k) * 16
                out_ref[row : row + 16, :] = both
    loads[5].wait()


def swap_index(rows, axis, unit):
    size = rows[0].shape[axis]
    index = lax.broadcasted_iota(jnp.int32, rows[0].shape, axis) // unit
    rows = list(rows)
    for bit in (2, 1):
        keep = (index & bit) == 0
        for n in range(4):
            if n & bit == 0:
                low, high = rows[n], rows[n + bit]
                rows[n] = jnp.where(keep, low, pltpu.roll(high, bit * unit, axis))
                rows[n + bit] = jnp.where(keep, pltpu.roll(low, size - bit * unit, axis), high)
    return rows


def swap_middle(rows):
    return [rows[0], rows[2], rows[1], rows[3]]


def legendre_kernel(x_ref, table_ref, scale_ref, spectra_ref, out_ref, rows_ref, back_ref):
    pairs, degrees, half_lat = table_ref.shape
    columns = spectra_ref.shape[1]
    slots = pairs // 2
    groups = half_lat // 128
    half = x_ref.shape[0] // 2
    tile = 16

    def fold(at, g):
        north, south = [], []
        for part in range(4):
            row = (4 * g + part) * columns + at
            north.append(x_ref[row : row + tile, :].astype(F32))
            south.append(x_ref[half + row : half + row + tile, :].astype(F32))
        for a in range(2):
            both = [n + t if a == 0 else n - t for n, t in zip(north, south)]
            done = []
            for h in (0, 8):
                by_column = swap_middle(swap_index([v[h : h + 8] for v in both], 1, 32))
                done.append(swap_index(by_column, 0, 1))
            for s in range(slots):
                rows_ref[2 * s + a, at : at + tile, 128 * g : 128 * g + 128] = jnp.concatenate(
                    [done[0][s], done[1][s]], axis=0
                ).astype(BF16)

    def unfold(at, g):
        view = (slice(at, at + tile), slice(128 * g, 128 * g + 128))
        even = [back_ref[(2 * s, *view)] for s in range(slots)]
        odd = [back_ref[(2 * s + 1, *view)] for s in range(slots)]
        for base in (0, half):
            both = [e + o if base == 0 else e - o for e, o in zip(even, odd)]
            done = []
            for h in (0, 8):
                by_column = swap_middle(swap_index([v[h : h + 8] for v in both], 0, 1))
                done.append(swap_index(by_column, 1, 32))
            for part in range(4):
                row = base + (4 * g + part) * columns + at
                out_ref[row : row + tile, :] = jnp.concatenate([done[0][part], done[1][part]], axis=0).astype(BF16)

    for g in range(groups):
        for at in range(0, columns, tile):
            fold(at, g)
    for sa in range(pairs):
        coefficient = dot(rows_ref[sa], table_ref[sa], NT)
        diffused = (coefficient * scale_ref[sa]).astype(BF16)
        spectra_ref[sa] = diffused
        back_ref[sa] = dot(diffused, table_ref[sa], NN)
    for g in range(groups):
        for at in range(0, columns, tile):
            unfold(at, g)


def inverse_kernel(in_ref, select_ref, trig_ref, out_hbm, w_ref, out_ref, sems):
    rows, lon_count = out_ref.shape
    waves = select_ref.shape[0]
    span = trig_ref.shape[1]
    per = waves // RADIX
    upper = lax.broadcasted_iota(jnp.int32, (8, 2 * rows), 0) < 4
    size = in_ref.shape[0] * 4 // waves

    def summed(n):
        acc = None
        for row in range(n * size, (n + 1) * size, 16):
            both = in_ref[row : row + 16, :].astype(F32)
            both = both[:8] + both[8:]
            acc = both if acc is None else acc + both
        return acc + pltpu.roll(acc, 4, 0)

    slots = [jnp.where(upper, summed(2 * n), summed(2 * n + 1)) for n in range(waves // 8)]
    slots = jnp.concatenate(slots, axis=0).T.astype(BF16)

    def ordered(i0, count):
        part = select_ref[i0 : i0 + count, :]
        both = dot(slots, jnp.concatenate([part, part], axis=0), NT)
        lane = lax.broadcasted_iota(jnp.int32, (rows, 2 * count), 1)
        return both[:rows], both[rows:], lane

    for p in range(3):
        wide = 2 * per
        real, imag, lane = ordered(p * wide, wide)
        imag = jnp.where((lane & per) == 0, imag, -imag)
        first = lane < wide
        g = jnp.concatenate([jnp.where(first, real, -imag), jnp.where(first, imag, real)], axis=0).astype(BF16)
        w = dot(g, trig_ref[2 * p * wide : 2 * (p + 1) * wide, :], NN)
        w_ref[2 * p] = w[:rows]
        w_ref[2 * p + 1] = w[rows:]
    for p in range(2):
        i0 = (6 + p) * per
        real, imag, lane = ordered(i0, per)
        g = jnp.where(lane < per, real, -imag).astype(BF16)
        w_ref[6 + p] = dot(g, trig_ref[2 * i0 : 2 * (i0 + per), :], NN)

    tile = 16
    width = 256

    def rows_copy(step):
        at = pl.ds(pl.multiple_of(step * tile, tile), tile)
        return pltpu.make_async_copy(out_ref.at[at], out_hbm.at[at], sems.at[step])

    def spread_rows(step, carry):
        r0 = pl.multiple_of(step * tile, tile)
        for x0 in range(0, span, width):
            p1, q1, p2, q2, p3, q3, p0, p4 = (w_ref[n, pl.ds(r0, tile), x0 : x0 + width] for n in range(8))
            e0 = p0 + p4
            e1 = p0 - p4
            plus = e0 + p2
            minus = e0 - p2
            low = e1 - q2
            high = e1 + q2
            t0 = p1 + p3
            t2 = q3 - q1
            t1 = HALF_ROOT * ((p1 - q1) - (p3 + q3))
            t3 = HALF_ROOT * ((p3 - q3) - (p1 + q1))
            pieces = (plus + t0, low + t1, minus + t2, high + t3, plus - t0, low - t1, minus - t2, high - t3)
            for b, piece in enumerate(pieces):
                out_ref[pl.ds(r0, tile), b * span + x0 : b * span + x0 + width] = piece.astype(BF16)
        rows_copy(step).start()
        return carry

    lax.fori_loop(0, rows // tile, spread_rows, 0)
    for step in range(rows // tile):
        rows_copy(step).wait()


VMEM = pl.BlockSpec(memory_space=pltpu.VMEM)
HBM = pl.BlockSpec(memory_space=pltpu.HBM)


def in_vmem(array):
    return pltpu.with_memory_space_constraint(array, pltpu.VMEM)


def in_hbm(array):
    return pltpu.with_memory_space_constraint(array, pltpu.HBM)


def call(body, name, outs, specs, scratch, out_specs=None):
    if out_specs is None:
        out_specs = tuple(VMEM for _ in outs)
    return pl.pallas_call(
        body,
        name=name,
        out_shape=outs,
        in_specs=specs,
        out_specs=out_specs,
        scratch_shapes=scratch,
        compiler_params=pltpu.CompilerParams(vmem_limit_bytes=16 << 20),
    )


def on_device(fields, legendre, damping, assignment, truncation):
    field_count, lat_rows, lon_count = fields.shape
    wave_slots, _, pair_slots, half_lat = legendre.shape
    total_waves = assignment.shape[0]
    lat_devices = lax.axis_size("lat")
    fld_devices = lax.axis_size("fld")
    field_total = damping.shape[0]
    rows = field_count * lat_rows
    columns = 2 * field_total
    pairs = 2 * wave_slots
    top = total_waves + 2 * pair_slots * fld_devices - 1
    span = lon_count // RADIX
    steps = rows // 16
    total = fld_devices * total_waves
    message = pltpu.VMEM((total, 2 * rows), BF16)

    def exchange(array):
        array = array.reshape(lat_devices * fld_devices, wave_slots, 2 * rows)
        return in_vmem(lax.all_to_all(array, ("lat", "fld"), 0, 0, tiled=True).reshape(total, 2 * rows))


    scalars = lambda array: in_hbm(array.reshape(1, array.shape[0]))
    sent, select, trig, table, scale = call(
        lambda *refs: forward_kernel(*refs, top=top), "forward",
        (
            message,
            pltpu.VMEM((total_waves, total_waves), BF16),
            pltpu.VMEM((2 * total_waves, span), BF16),
            pltpu.VMEM((pairs, pair_slots, half_lat), BF16),
            pltpu.VMEM((pairs, columns, pair_slots), F32),
        ),
        [HBM] * 6,
        [
            pltpu.VMEM((rows, lon_count), BF16),
            pltpu.VMEM((RADIX, rows, span), BF16),
            pltpu.VMEM((1, total_waves), jnp.int32),
            pltpu.SMEM((1, field_total), F32),
            pltpu.SMEM((1, total_waves), jnp.int32),
            pltpu.SMEM((1, total_waves), jnp.int32),
            pltpu.SemaphoreType.DMA((steps + 6,)),
        ],
    )(
        in_hbm(fields.reshape(rows, lon_count)),
        scalars(assignment),
        in_hbm(wave_table(total_waves, lon_count)),
        in_hbm(legendre.reshape(pairs, pair_slots, half_lat)),
        scalars(damping),
        scalars(truncation),
    )
    spectra, partial = call(
        legendre_kernel, "legendre", (jax.ShapeDtypeStruct((pairs, columns, pair_slots), BF16), message),
        [VMEM] * 3, [pltpu.VMEM((pairs, columns, half_lat), BF16), pltpu.VMEM((pairs, columns, half_lat), F32)],
    )(exchange(sent), in_vmem(table), in_vmem(scale))
    (field_out,) = call(
        inverse_kernel, "inverse", (jax.ShapeDtypeStruct((rows, lon_count), BF16),), [VMEM] * 3,
        [
            pltpu.VMEM((RADIX, rows, span), F32),
            pltpu.VMEM((rows, lon_count), BF16),
            pltpu.SemaphoreType.DMA((steps,)),
        ],
        (HBM,),
    )(exchange(partial), in_vmem(select), in_vmem(trig))
    return (
        field_out.reshape(field_count, lat_rows, lon_count),
        spectra.reshape(wave_slots, 2, field_total, 2, pair_slots),
    )


def solution(mesh):
    placed = (P("fld", "lat", None), P("lat", None, "fld", None), P(), P(), P())
    return jax.shard_map(
        on_device,
        mesh=mesh,
        in_specs=placed,
        out_specs=(P("fld", "lat", None), P("lat", None, None, None, "fld")),
        check_vma=False,
    )
```

```python
import math

import jax
import jax.numpy as jnp
import numpy as np
from jax import lax
from jax.experimental import pallas as pl
from jax.experimental.pallas import tpu as pltpu
from jax.sharding import PartitionSpec as P

F32 = jnp.float32
BF16 = jnp.bfloat16
RADIX = 8
HALF_ROOT = math.sqrt(0.5)
NT = (((1,), (1,)), ((), ()))
NN = (((1,), (0,)), ((), ()))
CLASS_ORDER = (1, 7, 2, 6, 3, 5, 8, 4)


def dot(a, b, dims):
    return lax.dot_general(a, b, dims, preferred_element_type=F32)


def wave_table(total_waves, lon_count):
    span = lon_count // RADIX
    per = total_waves // RADIX
    factor = math.sqrt(2.0 / lon_count)
    blocks = []
    for classes in ((1, 7), (2, 6), (3, 5), (8,), (4,)):
        waves = np.concatenate([RADIX * np.arange(per) + c for c in classes])
        angle = (waves[:, None] * np.arange(span)[None, :] % lon_count) * (2.0 * np.pi / lon_count)
        sign = np.where(np.arange(len(waves)) < per, 1.0, -1.0)[:, None]
        blocks += [factor * np.cos(angle), factor * sign * np.sin(angle)]
    return jnp.asarray(np.concatenate(blocks).astype(np.float32), BF16)


def forward_kernel(
    fields_hbm, assign_hbm, trig_hbm, table_hbm, damping_hbm, limit_hbm,
    out_ref, select_ref, trig_ref, table_ref, scale_ref,
    fields_ref, z_ref, assign_ref, damping_ref, slot_ref, limit_ref, sems, *, top,
):
    rows, lon_count = fields_ref.shape
    waves = select_ref.shape[0]
    span = trig_ref.shape[1]
    per = waves // RADIX
    tile = 16
    width = 256
    steps = rows // tile

    def rows_copy(step):
        at = pl.ds(pl.multiple_of(step * tile, tile), tile)
        return pltpu.make_async_copy(fields_hbm.at[at], fields_ref.at[at], sems.at[step])

    moves = (
        (damping_hbm, damping_ref), (assign_hbm, slot_ref), (limit_hbm, limit_ref), (assign_hbm, assign_ref),
        (trig_hbm, trig_ref), (table_hbm, table_ref),
    )
    loads = [pltpu.make_async_copy(*move, sems.at[steps + n]) for n, move in enumerate(moves)]
    for load in loads[:4]:
        load.start()
    for step in range(steps):
        rows_copy(step).start()
    loads[4].start()
    loads[5].start()

    def fold_rows(step, carry):
        r0 = pl.multiple_of(step * tile, tile)
        rows_copy(step).wait()
        for x0 in range(0, span, width):
            s = []
            for b in range(RADIX):
                v = fields_ref[pl.ds(r0, tile), b * span + x0 : b * span + x0 + width].astype(F32)
                s.append(v * v)
            e = [s[b] + s[b + 4] for b in range(4)]
            o = [s[b] - s[b + 4] for b in range(4)]
            u = HALF_ROOT * (o[1] - o[3])
            v = HALF_ROOT * (o[1] + o[3])
            even = e[0] + e[2]
            odd = e[1] + e[3]
            parts = (
                o[0] + u, -(o[2] + v),
                e[0] - e[2], e[3] - e[1],
                o[0] - u, o[2] - v,
                even + odd, even - odd,
            )
            for n, part in enumerate(parts):
                z_ref[n, pl.ds(r0, tile), x0 : x0 + width] = part.astype(BF16)
        return carry

    lax.fori_loop(0, steps, fold_rows, 0)
    for load in loads[:4]:
        load.wait()

    pairs, columns, degrees = scale_ref.shape
    slots = pairs // 2
    slot0 = lax.axis_index("lat") * slots
    first = lax.axis_index("fld") * degrees
    field = lax.broadcasted_iota(jnp.int32, (columns, degrees), 0) // 2
    damp = jnp.zeros((columns, degrees), F32)
    for n in range(columns // 2):
        damp = jnp.where(field == n, damping_ref[0, n], damp)
    pair_index = first + lax.broadcasted_iota(jnp.int32, (8, degrees), 1)
    for s in range(slots):
        wave = slot_ref[0, slot0 + s]
        limit = limit_ref[0, wave]
        for a in range(2):
            offset = 2 * pair_index + a
            degree = (wave + 1 + offset).astype(F32)
            ratio = degree * (degree + 1.0) / float(top * (top + 1))
            square = ratio * ratio
            kept = offset < limit
            for c in range(0, columns, 8):
                factor = 0.5 / (1.0 + damp[c : c + 8] * square)
                scale_ref[2 * s + a, c : c + 8, :] = jnp.where(kept, factor, 0.0)

    wave_of = RADIX * lax.broadcasted_iota(jnp.int32, (per, waves), 0) - 1
    for n, cls in enumerate(CLASS_ORDER):
        hit = (wave_of + cls) == assign_ref[...]
        select_ref[n * per : (n + 1) * per, :] = jnp.where(hit, 1.0, 0.0).astype(BF16)

    loads[4].wait()
    acc = jnp.zeros((2 * rows, waves), F32)
    for p in range(3):
        wide = 2 * per
        zz = z_ref[2 * p : 2 * p + 2].reshape(2 * rows, span)
        d = dot(zz, trig_ref[2 * p * wide : 2 * (p + 1) * wide, :], NT)
        turned = pltpu.roll(d, wide, 1)
        real = d[:rows] + turned[rows:]
        imag = d[rows:] - turned[:rows]
        lane = lax.broadcasted_iota(jnp.int32, imag.shape, 1)
        imag = jnp.where((lane & per) == 0, imag, -imag)
        both = jnp.concatenate([real, imag], axis=0).astype(BF16)[:, :wide]
        acc = acc + dot(both, select_ref[p * wide : (p + 1) * wide, :], NN)
    for p in range(2):
        i0 = (6 + p) * per
        d = dot(z_ref[6 + p], trig_ref[2 * i0 : 2 * (i0 + per), :], NT)
        both = jnp.concatenate([d[:, :per], -d[:, per:]], axis=0).astype(BF16)
        acc = acc + dot(both, select_ref[i0 : i0 + per, :], NN)
    by_slot = acc.T
    upper = lax.broadcasted_iota(jnp.int32, (8, 2 * rows), 0) < 4
    repeats = out_ref.shape[0] // (4 * waves)
    for n in range(waves // 8):
        group = by_slot[8 * n : 8 * n + 8]
        turned = pltpu.roll(group, 4, 0)
        for m, both in enumerate((jnp.where(upper, group, turned), jnp.where(upper, turned, group))):
            both = jnp.concatenate([both, both], axis=0).astype(BF16)
            for k in range(repeats):
                row = ((2 * n + m) * repeats + k) * 16
                out_ref[row : row + 16, :] = both
    loads[5].wait()


def swap_index(rows, axis, unit):
    size = rows[0].shape[axis]
    index = lax.broadcasted_iota(jnp.int32, rows[0].shape, axis) // unit
    rows = list(rows)
    for bit in (2, 1):
        keep = (index & bit) == 0
        for n in range(4):
            if n & bit == 0:
                low, high = rows[n], rows[n + bit]
                rows[n] = jnp.where(keep, low, pltpu.roll(high, bit * unit, axis))
                rows[n + bit] = jnp.where(keep, pltpu.roll(low, size - bit * unit, axis), high)
    return rows


def swap_middle(rows):
    return [rows[0], rows[2], rows[1], rows[3]]


def legendre_kernel(x_ref, table_ref, scale_ref, spectra_ref, out_ref, rows_ref, back_ref):
    pairs, degrees, half_lat = table_ref.shape
    columns = spectra_ref.shape[1]
    slots = pairs // 2
    groups = half_lat // 128
    half = x_ref.shape[0] // 2
    tile = 16

    def fold(at, g):
        north, south = [], []
        for part in range(4):
            row = (4 * g + part) * columns + at
            north.append(x_ref[row : row + tile, :].astype(F32))
            south.append(x_ref[half + row : half + row + tile, :].astype(F32))
        for a in range(2):
            both = [n + t if a == 0 else n - t for n, t in zip(north, south)]
            done = []
            for h in (0, 8):
                by_column = swap_middle(swap_index([v[h : h + 8] for v in both], 1, 32))
                done.append(swap_index(by_column, 0, 1))
            for s in range(slots):
                rows_ref[2 * s + a, at : at + tile, 128 * g : 128 * g + 128] = jnp.concatenate(
                    [done[0][s], done[1][s]], axis=0
                ).astype(BF16)

    def unfold(at, g):
        lanes = slice(128 * g, 128 * g + 128)
        done = ([], [])
        for h in (0, 8):
            lines = slice(at + h, at + h + 8)
            even = [back_ref[2 * s, lines, lanes] for s in range(slots)]
            odd = [back_ref[2 * s + 1, lines, lanes] for s in range(slots)]
            for n in range(2):
                both = [e + o if n == 0 else e - o for e, o in zip(even, odd)]
                done[n].append(swap_index(swap_middle(swap_index(both, 0, 1)), 1, 32))
        for n in range(2):
            for part in range(4):
                row = n * half + (4 * g + part) * columns + at
                pair = [moved[part] for moved in done[n]]
                out_ref[row : row + tile, :] = jnp.concatenate(pair, axis=0).astype(BF16)

    for g in range(groups):
        for at in range(0, columns, tile):
            fold(at, g)
    coefficients = [dot(rows_ref[sa], table_ref[sa], NT) for sa in range(pairs)]
    for sa in range(pairs):
        diffused = (coefficients[sa] * scale_ref[sa]).astype(BF16)
        spectra_ref[sa] = diffused
        back_ref[sa] = dot(diffused, table_ref[sa], NN)
    for g in range(groups):
        for at in range(0, columns, tile):
            unfold(at, g)


def inverse_kernel(in_ref, select_ref, trig_ref, out_hbm, w_ref, out_ref, sems):
    rows, lon_count = out_ref.shape
    waves = select_ref.shape[0]
    span = trig_ref.shape[1]
    per = waves // RADIX
    upper = lax.broadcasted_iota(jnp.int32, (8, 2 * rows), 0) < 4
    size = in_ref.shape[0] * 4 // waves

    def summed(n):
        acc = None
        for row in range(n * size, (n + 1) * size, 16):
            both = in_ref[row : row + 16, :].astype(F32)
            both = both[:8] + both[8:]
            acc = both if acc is None else acc + both
        return acc + pltpu.roll(acc, 4, 0)

    slots = [jnp.where(upper, summed(2 * n), summed(2 * n + 1)) for n in range(waves // 8)]
    slots = jnp.concatenate(slots, axis=0).T.astype(BF16)

    def ordered(i0, count):
        part = select_ref[i0 : i0 + count, :]
        both = dot(slots, jnp.concatenate([part, part], axis=0), NT)
        lane = lax.broadcasted_iota(jnp.int32, (rows, 2 * count), 1)
        return both[:rows], both[rows:], lane

    for p in range(3):
        wide = 2 * per
        real, imag, lane = ordered(p * wide, wide)
        imag = jnp.where((lane & per) == 0, imag, -imag)
        first = lane < wide
        g = jnp.concatenate([jnp.where(first, real, -imag), jnp.where(first, imag, real)], axis=0).astype(BF16)
        w = dot(g, trig_ref[2 * p * wide : 2 * (p + 1) * wide, :], NN)
        w_ref[2 * p] = w[:rows]
        w_ref[2 * p + 1] = w[rows:]
    for p in range(2):
        i0 = (6 + p) * per
        real, imag, lane = ordered(i0, per)
        g = jnp.where(lane < per, real, -imag).astype(BF16)
        w_ref[6 + p] = dot(g, trig_ref[2 * i0 : 2 * (i0 + per), :], NN)

    tile = 16
    width = 256

    def rows_copy(step):
        at = pl.ds(pl.multiple_of(step * tile, tile), tile)
        return pltpu.make_async_copy(out_ref.at[at], out_hbm.at[at], sems.at[step])

    def spread_rows(step, carry):
        r0 = pl.multiple_of(step * tile, tile)
        for x0 in range(0, span, width):
            p1, q1, p2, q2, p3, q3, p0, p4 = (w_ref[n, pl.ds(r0, tile), x0 : x0 + width] for n in range(8))
            e0 = p0 + p4
            e1 = p0 - p4
            plus = e0 + p2
            minus = e0 - p2
            low = e1 - q2
            high = e1 + q2
            t0 = p1 + p3
            t2 = q3 - q1
            t1 = HALF_ROOT * ((p1 - q1) - (p3 + q3))
            t3 = HALF_ROOT * ((p3 - q3) - (p1 + q1))
            pieces = (plus + t0, low + t1, minus + t2, high + t3, plus - t0, low - t1, minus - t2, high - t3)
            for b, piece in enumerate(pieces):
                out_ref[pl.ds(r0, tile), b * span + x0 : b * span + x0 + width] = piece.astype(BF16)
        rows_copy(step).start()
        return carry

    lax.fori_loop(0, rows // tile, spread_rows, 0)
    for step in range(rows // tile):
        rows_copy(step).wait()


VMEM = pl.BlockSpec(memory_space=pltpu.VMEM)
HBM = pl.BlockSpec(memory_space=pltpu.HBM)


def in_vmem(array):
    return pltpu.with_memory_space_constraint(array, pltpu.VMEM)


def in_hbm(array):
    return pltpu.with_memory_space_constraint(array, pltpu.HBM)


def call(body, name, outs, specs, scratch, out_specs=None):
    if out_specs is None:
        out_specs = tuple(VMEM for _ in outs)
    return pl.pallas_call(
        body,
        name=name,
        out_shape=outs,
        in_specs=specs,
        out_specs=out_specs,
        scratch_shapes=scratch,
        compiler_params=pltpu.CompilerParams(vmem_limit_bytes=16 << 20),
    )


def on_device(fields, legendre, damping, assignment, truncation):
    field_count, lat_rows, lon_count = fields.shape
    wave_slots, _, pair_slots, half_lat = legendre.shape
    total_waves = assignment.shape[0]
    lat_devices = lax.axis_size("lat")
    fld_devices = lax.axis_size("fld")
    field_total = damping.shape[0]
    rows = field_count * lat_rows
    columns = 2 * field_total
    pairs = 2 * wave_slots
    top = total_waves + 2 * pair_slots * fld_devices - 1
    span = lon_count // RADIX
    steps = rows // 16
    total = fld_devices * total_waves
    message = pltpu.VMEM((total, 2 * rows), BF16)

    def exchange(array):
        array = array.reshape(lat_devices * fld_devices, wave_slots, 2 * rows)
        return in_vmem(lax.all_to_all(array, ("lat", "fld"), 0, 0, tiled=True).reshape(total, 2 * rows))


    scalars = lambda array: in_hbm(array.reshape(1, array.shape[0]))
    sent, select, trig, table, scale = call(
        lambda *refs: forward_kernel(*refs, top=top), "forward",
        (
            message,
            pltpu.VMEM((total_waves, total_waves), BF16),
            pltpu.VMEM((2 * total_waves, span), BF16),
            pltpu.VMEM((pairs, pair_slots, half_lat), BF16),
            pltpu.VMEM((pairs, columns, pair_slots), F32),
        ),
        [HBM] * 6,
        [
            pltpu.VMEM((rows, lon_count), BF16),
            pltpu.VMEM((RADIX, rows, span), BF16),
            pltpu.VMEM((1, total_waves), jnp.int32),
            pltpu.SMEM((1, field_total), F32),
            pltpu.SMEM((1, total_waves), jnp.int32),
            pltpu.SMEM((1, total_waves), jnp.int32),
            pltpu.SemaphoreType.DMA((steps + 6,)),
        ],
    )(
        in_hbm(fields.reshape(rows, lon_count)),
        scalars(assignment),
        in_hbm(wave_table(total_waves, lon_count)),
        in_hbm(legendre.reshape(pairs, pair_slots, half_lat)),
        scalars(damping),
        scalars(truncation),
    )
    spectra, partial = call(
        legendre_kernel, "legendre", (jax.ShapeDtypeStruct((pairs, columns, pair_slots), BF16), message),
        [VMEM] * 3, [pltpu.VMEM((pairs, columns, half_lat), BF16), pltpu.VMEM((pairs, columns, half_lat), F32)],
    )(exchange(sent), in_vmem(table), in_vmem(scale))
    (field_out,) = call(
        inverse_kernel, "inverse", (jax.ShapeDtypeStruct((rows, lon_count), BF16),), [VMEM] * 3,
        [
            pltpu.VMEM((RADIX, rows, span), F32),
            pltpu.VMEM((rows, lon_count), BF16),
            pltpu.SemaphoreType.DMA((steps,)),
        ],
        (HBM,),
    )(exchange(partial), in_vmem(select), in_vmem(trig))
    return (
        field_out.reshape(field_count, lat_rows, lon_count),
        spectra.reshape(wave_slots, 2, field_total, 2, pair_slots),
    )


def solution(mesh):
    placed = (P("fld", "lat", None), P("lat", None, "fld", None), P(), P(), P())
    return jax.shard_map(
        on_device,
        mesh=mesh,
        in_specs=placed,
        out_specs=(P("fld", "lat", None), P("lat", None, None, None, "fld")),
        check_vma=False,
    )
```
